128 devices in a mesh: grp: 4 (over z_lo, core), dev: 32 (over y, z_hi, x).
Axes of the slice: x: 4, y: 4, z: 4 (z_hi: 2, z_lo: 2; z = z_hi * 2 + z_lo), core: 2. Of those that a mesh axis runs over, the one named last changes fastest.
Arguments:
- tokens: bfloat16 [16384, 2048], P(('grp', 'dev')), may hold values from -6 to 6
- queries: bfloat16 [16384, 2048], P(('grp', 'dev')), may hold values from -7.5 to 7.5
- suffix_keys: bfloat16 [16384, 2048], P(('grp', 'dev')), may hold values from -6 to 6
- suffix_values: bfloat16 [16384, 2048], P(('grp', 'dev')), may hold values from -6 to 6
- prefix_keys: bfloat16 [4, 1024, 2048], P('grp', 'dev'), may hold values from -6 to 6
- prefix_values: bfloat16 [4, 1024, 2048], P('grp', 'dev'), may hold values from -6 to 6
- out_weight: bfloat16 [2048, 2048], replicated, may hold values from -0.125 to 0.125
- norm_gain: float32 [2048], replicated, may hold values from 0.1 to 1.9
- routes: int32 [16384, 6], P(('grp', 'dev')), may hold values from 0 to 63, all different within a row; in each aligned block of 128 rows (0 to 127, 128 to 255, ...) at most 16 rows name the same one
- route_weights: float32 [16384, 6], P(('grp', 'dev')), may hold values from 0.05 to 0.5
- gate_up_weight: bfloat16 [128, 2048, 1408], P(('grp', 'dev')), may hold values from -0.125 to 0.125
- down_weight: bfloat16 [128, 704, 2048], P(('grp', 'dev')), may hold values from -0.15625 to 0.15625
Outputs:
- attended: bfloat16 [16384, 2048], P(('grp', 'dev'))
- routed: bfloat16 [16384, 2048], P(('grp', 'dev'))
The draws below stay inside these ranges and needn't reach their ends.
Inputs may be any that keep to these rules, and one draw needn't show every extreme that they name: `routes`: each row names 6 different experts. Within the rows of one request (aligned blocks of 128 rows) no expert is named by more than 16 rows, and in some block one expert is named exactly 16 times.
All inputs are finite; a program needn't handle non-finite values.
Results may differ from the reference program's by a relative error of at most 0.019.
Values may be sent and summed in bfloat16 or wider, within the bound.
A program may use at most 128 MiB of HBM per device.

```python
import math
import jax
import jax.numpy as jnp
import numpy as np
from jax import lax

D = 2048
HEADS = 16
HEAD_DIM = 128
FF = 1408
TOP = 6
TOK_DEV = 128
EXPERTS = 64
HALF = 704
CAP = 16
PREFIX = 1024
GROUPS = 4
TOKENS = 16384


def draw_queries(key, part):
    inner = jax.random.fold_in(key, 17)
    values = jnp.clip(1.5 * jax.random.normal(inner, (TOKENS, D), jnp.float32), -7.5, 7.5)
    return values.astype(jnp.bfloat16)


def draw_prefix_keys(key, part):
    inner = jax.random.fold_in(key, 29)
    values = jnp.clip(jax.random.normal(inner, (GROUPS, PREFIX, D), jnp.float32), -6.0, 6.0)
    return values.astype(jnp.bfloat16)


def level_of(rng, dims, split, least, top_value):
    factor_of = 1.0
    for axis_at, parts in split:
        heights = jax.random.uniform(jax.random.fold_in(jax.random.fold_in(rng, 6), axis_at), (parts,), jnp.float32, least / len(split), top_value / len(split))
        factor_of = factor_of * jnp.repeat(jnp.exp(heights), dims[axis_at] // parts).reshape((-1,) + (1,) * (len(dims) - 1 - axis_at))
    return factor_of


def shared_out(own_key, own, number, rows, amount, top, reach, lean):
    order = jax.random.permutation(own_key, amount)
    packed, ordinary = load_shares(amount, rows * top, reach, lean, True), load_shares(amount, rows * top, reach, lean, False)
    places = jnp.arange(amount)

    def named(tallies, rotation):
        used = int((tallies > 0).sum())
        fixed = max(1, used // 4)
        moved = fixed + (places - fixed + rotation * (used - fixed)) % max(1, amount - fixed)
        return jnp.zeros((amount,), jnp.int32).at[order[jnp.where(places < fixed, places, moved)]].set(jnp.asarray(tallies, jnp.int32))

    tallies = jnp.where(number % 4 == 0, named(packed, number // 4), named(ordinary, number - number // 4 - 1))
    mixed = jax.random.permutation(jax.random.fold_in(own, 3), amount)
    donor, receiver = mixed[0:amount // 2 * 2:2], mixed[1:amount // 2 * 2:2]
    slack = jnp.minimum(tallies[donor] - 1, reach - tallies[receiver]) // 2
    slack = jnp.where((donor == order[0]) | (receiver == order[0]) | (tallies[receiver] == 0), 0, jnp.maximum(slack, 0))
    moved = jax.random.randint(jax.random.fold_in(own, 4), (amount // 2,), 0, 1 << 20) % (slack + 1)
    tallies = tallies.at[donor].add(-moved).at[receiver].add(moved)
    members = jnp.searchsorted(jnp.cumsum(tallies), jnp.arange(rows * top), side="right").astype(jnp.int32)
    table = members.reshape(top, rows).T
    table = table[jax.random.permutation(jax.random.fold_in(own, 1), rows)]
    rotation = jax.random.randint(jax.random.fold_in(own, 2), (rows, 1), 0, top)
    return jnp.take_along_axis(table, (jnp.arange(top)[None, :] + rotation) % top, axis=1)


def load_shares(count, total, reach, skew, full):
    weights = [(1 << 20) // math.isqrt(standing ** skew) + 1 for standing in range(1, count + 1)]
    largest = reach if full else min(reach, max(-(-total // count), total * weights[0] // sum(weights)))
    least = 1 if total - largest >= count - 1 else 0
    holding, spare = [largest] + [least] * (count - 1), total - largest - least * (count - 1)
    while spare > 0:
        free = [i for i in range(1, count) if holding[i] < largest] or [i for i in range(1, count) if holding[i] < reach]
        mass, budget = sum([weights[i] for i in free]), spare
        for i in free:
            extra = min(reach - holding[i], max(1, budget * weights[i] // mass), spare)
            holding[i] = holding[i] + extra
            spare = spare - extra
    return np.array(holding)


def gaussian(own_key, dims, width, most, cuts=(), held_as=jnp.bfloat16):
    level = level_of(own_key, dims, cuts, -0.22, 0.18) if cuts else 1.0
    drawn = jax.random.normal(own_key, dims, jnp.float32) * width * level
    return jnp.minimum(jnp.maximum(drawn, -most), most).astype(held_as)


def setup_inputs(seed: int = 0) -> dict:
    key_of = jax.random.split(jax.random.key(seed), 13)
    tokens = gaussian(key_of[0], (TOKENS, D), 1.0, 6.0, ((0, 128),))
    queries = draw_queries(jax.random.fold_in(key_of[12], 71), 0)
    suffix_keys = gaussian(key_of[2], (TOKENS, D), 1.0, 6.0, ((0, 128),))
    suffix_values = gaussian(key_of[3], (TOKENS, D), 1.0, 6.0, ((0, 128),))
    prefix_keys = draw_prefix_keys(jax.random.fold_in(key_of[12], 71), 0)
    prefix_values = gaussian(key_of[5], (GROUPS, PREFIX, D), 1.0, 6.0, ((0, 4), (1, 32)))
    out_weight = gaussian(key_of[6], (D, D), D ** -0.5, 0.125)
    norm_gain = jnp.clip(1.0 + 0.18 * jax.random.normal(key_of[7], (D,), jnp.float32), 0.1, 1.9)
    routes_keys = jax.random.split(jax.random.fold_in(key_of[8], 1), TOKENS // TOK_DEV)
    routes_turns = jax.random.permutation(jax.random.fold_in(key_of[8], 3), TOKENS // TOK_DEV)
    routes = jax.vmap(lambda own, number: shared_out(jax.random.fold_in(key_of[8], 2), own, number, TOK_DEV, EXPERTS, TOP, CAP, 2))(routes_keys, routes_turns).reshape((TOKENS, TOP))
    route_weights = jnp.clip(jnp.exp(math.log(0.5) - 2.3025851 * jax.random.uniform(key_of[9], (TOKENS, TOP), jnp.float32) ** level_of(key_of[9], (TOKENS, TOP), ((0, 128),), -0.2, 0.2)), 0.05, 0.5)
    gate_up_weight = gaussian(key_of[10], (2 * EXPERTS, D, 2 * HALF), D ** -0.5, 0.125, ((0, 128),))
    down_weight = gaussian(key_of[11], (2 * EXPERTS, HALF, D), FF ** -0.5, 0.15625, ((0, 128),))
    return {"tokens": tokens, "queries": queries, "suffix_keys": suffix_keys, "suffix_values": suffix_values, "prefix_keys": prefix_keys, "prefix_values": prefix_values, "out_weight": out_weight, "norm_gain": norm_gain, "routes": routes, "route_weights": route_weights, "gate_up_weight": gate_up_weight, "down_weight": down_weight}


def half_expert(rows, gate_up, down_proj):
    hidden_units = down_proj.shape[0]
    projected = jnp.dot(rows, gate_up, preferred_element_type=jnp.float32)
    active = (jax.nn.silu(projected[:, :hidden_units]) * projected[:, hidden_units:]).astype(jnp.bfloat16)
    return jnp.dot(active, down_proj, preferred_element_type=jnp.float32).astype(jnp.bfloat16)

def attention_part(query_heads, key_rows, value_rows, allowed):
    key_heads = key_rows.astype(jnp.float32).reshape(-1, HEADS, HEAD_DIM)
    value_heads = value_rows.astype(jnp.float32).reshape(-1, HEADS, HEAD_DIM)
    scores = jnp.einsum('rhd,khd->hrk', query_heads, key_heads, precision=lax.Precision.HIGHEST) / math.sqrt(HEAD_DIM)
    scores = jnp.where(allowed[None], scores, -jnp.inf)
    row_max = lax.optimization_barrier(jnp.max(scores, axis=-1))
    shifted = jnp.exp(scores - row_max[..., None])
    row_sum = lax.optimization_barrier(jnp.sum(shifted, axis=-1))
    rounded = lax.optimization_barrier(shifted.astype(jnp.bfloat16)).astype(jnp.float32)
    weighted = jnp.einsum('hrk,khd->hrd', rounded, value_heads, precision=lax.Precision.HIGHEST)
    return (row_max, row_sum, weighted)

def reference(tokens, queries, suffix_keys, suffix_values, prefix_keys, prefix_values, out_weight, norm_gain, routes, route_weights, gate_up_weight, down_weight):
    requests_group = TOKENS // (TOK_DEV * GROUPS)
    causal = jnp.arange(TOK_DEV)[:, None] >= jnp.arange(TOK_DEV)[None, :]
    everything = jnp.ones((TOK_DEV, PREFIX), dtype=bool)

    def one_request(index):
        offset = (index * TOK_DEV).astype(jnp.int32)
        group = (index // requests_group).astype(jnp.int32)
        query_heads = lax.dynamic_slice_in_dim(queries, offset, TOK_DEV, 0).astype(jnp.float32).reshape(TOK_DEV, HEADS, HEAD_DIM)
        keys_before = lax.dynamic_index_in_dim(prefix_keys, group, 0, keepdims=False)
        values_before = lax.dynamic_index_in_dim(prefix_values, group, 0, keepdims=False)
        keys_after = lax.dynamic_slice_in_dim(suffix_keys, offset, TOK_DEV, 0)
        values_after = lax.dynamic_slice_in_dim(suffix_values, offset, TOK_DEV, 0)
        prefix_max, prefix_sum, prefix_acc = attention_part(query_heads, keys_before, values_before, everything)
        suffix_max, suffix_sum, suffix_acc = attention_part(query_heads, keys_after, values_after, causal)
        merged_max = jnp.maximum(prefix_max, suffix_max)
        prefix_scale = jnp.exp(prefix_max - merged_max)
        suffix_scale = jnp.exp(suffix_max - merged_max)
        mixed = (prefix_acc * prefix_scale[..., None] + suffix_acc * suffix_scale[..., None]) / (prefix_sum * prefix_scale + suffix_sum * suffix_scale)[..., None]
        heads_out = jnp.transpose(mixed, (1, 0, 2)).reshape(TOK_DEV, D).astype(jnp.bfloat16)
        return jnp.dot(heads_out, out_weight, preferred_element_type=jnp.float32).astype(jnp.bfloat16)
    attended = lax.map(one_request, jnp.arange(TOKENS // TOK_DEV, dtype=jnp.int32)).reshape(TOKENS, D)
    residual = tokens.astype(jnp.float32) + attended.astype(jnp.float32)
    mean_square = lax.optimization_barrier(jnp.mean(residual * residual, axis=-1, keepdims=True))
    normed = (residual * lax.rsqrt(mean_square + 1e-06) * norm_gain).astype(jnp.bfloat16)
    blocks = TOKENS // TOK_DEV
    flat_routes = routes.reshape(blocks, TOK_DEV * TOP)
    onehot = (flat_routes[..., None] == jnp.arange(EXPERTS, dtype=jnp.int32)).astype(jnp.int32)
    ranking = lax.optimization_barrier(jnp.sum(jnp.cumsum(onehot, axis=1) * onehot, axis=-1)) - 1
    slots = flat_routes * CAP + ranking
    owners = (jnp.arange(TOKENS * TOP, dtype=jnp.int32) // TOP).reshape(blocks, TOK_DEV * TOP)
    block_rows = jnp.arange(blocks, dtype=jnp.int32)[:, None]
    owner_table = jnp.full((blocks, EXPERTS * CAP), TOKENS, jnp.int32).at[block_rows, slots].set(owners)
    weight_table = jnp.zeros((blocks, EXPERTS * CAP), jnp.float32).at[block_rows, slots].set(route_weights.reshape(blocks, TOK_DEV * TOP))

    def expert_step(routed_sum, expert):
        begin = (expert * CAP).astype(jnp.int32)
        picked = lax.dynamic_slice_in_dim(owner_table, begin, CAP, 1).reshape(-1)
        gates = lax.dynamic_slice_in_dim(weight_table, begin, CAP, 1).reshape(-1)
        rows = jnp.take(normed, picked, axis=0, mode='fill', fill_value=0)
        first = half_expert(rows, lax.dynamic_index_in_dim(gate_up_weight, (2 * expert).astype(jnp.int32), 0, keepdims=False), lax.dynamic_index_in_dim(down_weight, (2 * expert).astype(jnp.int32), 0, keepdims=False))
        second = half_expert(rows, lax.dynamic_index_in_dim(gate_up_weight, (2 * expert + 1).astype(jnp.int32), 0, keepdims=False), lax.dynamic_index_in_dim(down_weight, (2 * expert + 1).astype(jnp.int32), 0, keepdims=False))
        output = lax.optimization_barrier((first.astype(jnp.float32) + second.astype(jnp.float32)).astype(jnp.bfloat16)).astype(jnp.float32)
        routed_sum = routed_sum.at[picked].add(output * gates[:, None], mode='drop')
        return (routed_sum, None)
    routed_sum, unused = lax.scan(expert_step, jnp.zeros((TOKENS, D), jnp.float32), jnp.arange(EXPERTS, dtype=jnp.int32))
    return (attended, routed_sum.astype(jnp.bfloat16))
```

```python
import functools
import math

import jax
import jax.numpy as jnp
from jax import lax
from jax.experimental import pallas as pl
from jax.experimental.pallas import tpu as pltpu
from jax.sharding import PartitionSpec as P

HEADS = 16
HEAD_DIM = 128
TOP = 6
MESH = pl.DeviceIdType.MESH
F32 = jnp.float32
BF16 = jnp.bfloat16
NT = (((1,), (1,)), ((), ()))


def attention_kernel(
    q_ref, k_ref, v_ref, sk_ref, sv_ref, tok_ref, gain_ref, ow_hbm,
    attended_ref, normed_ref,
    qbuf, kbuf, vbuf, osend, orecv, stsend, strecv, suf_acc, suf_stat, vt, hout, resid, ow,
    recv_sem, send_sem, ow_sem,
):
    me = lax.axis_index("dev")
    y, zh, x = me // 8, (me // 4) % 2, me % 4
    head = y * 4 + x
    scale = 1.0 / math.sqrt(HEAD_DIM)

    ow_copy = pltpu.make_async_copy(ow_hbm, ow, ow_sem)
    ow_copy.start()

    barrier = pltpu.get_barrier_semaphore()

    def greet(j, c):
        pl.semaphore_signal(barrier, inc=1, device_id={"dev": (me + j) % 32}, device_id_type=MESH)
        return c

    lax.fori_loop(1, 32, greet, 0)
    pl.semaphore_wait(barrier, 31)

    def columns(h):
        return pl.ds(pl.multiple_of(h * HEAD_DIM, HEAD_DIM), HEAD_DIM)

    def key_rows(d):
        return pl.ds(pl.multiple_of(d * 32, 32), 32)

    pltpu.make_async_copy(q_ref.at[:, columns(head)], qbuf.at[head], recv_sem.at[0]).start()
    pltpu.make_async_copy(k_ref.at[:, columns(head)], kbuf.at[key_rows(me), :], recv_sem.at[1]).start()
    pltpu.make_async_copy(v_ref.at[:, columns(head)], vbuf.at[key_rows(me), :], recv_sem.at[2]).start()

    def send_kv(j, c):
        dz, dy, dx = j // 16, (j // 4) % 4, j % 4
        ty, tz, tx = (y + dy) % 4, (zh + dz) % 2, (x + dx) % 4
        to = {"dev": ty * 8 + tz * 4 + tx}
        h = ty * 4 + tx
        pltpu.make_async_remote_copy(
            k_ref.at[:, columns(h)], kbuf.at[key_rows(me), :], send_sem.at[1], recv_sem.at[1],
            device_id=to, device_id_type=MESH,
        ).start()
        pltpu.make_async_remote_copy(
            v_ref.at[:, columns(h)], vbuf.at[key_rows(me), :], send_sem.at[2], recv_sem.at[2],
            device_id=to, device_id_type=MESH,
        ).start()
        return c

    def send_q(j, c):
        ty, tx = (y + j // 4) % 4, (x + j % 4) % 4
        h = ty * 4 + tx
        pltpu.make_async_remote_copy(
            q_ref.at[:, columns(h)], qbuf.at[head], send_sem.at[0], recv_sem.at[0],
            device_id={"dev": ty * 8 + zh * 4 + tx}, device_id_type=MESH,
        ).start()
        return c

    lax.fori_loop(1, 32, send_kv, 0)
    lax.fori_loop(1, 16, send_q, 0)

    key_at = lax.broadcasted_iota(jnp.int32, (128, 128), 0)
    query_at = lax.broadcasted_iota(jnp.int32, (128, 128), 1)
    allowed = key_at <= query_at
    for h in range(HEADS):
        cols = slice(h * HEAD_DIM, (h + 1) * HEAD_DIM)
        s = lax.dot_general(sk_ref[:, cols], q_ref[:, cols], NT, preferred_element_type=F32) * scale
        s = jnp.where(allowed, s, -jnp.inf)
        m = jnp.max(s, axis=0, keepdims=True)
        p = jnp.exp(s - m)
        suf_stat[0, h : h + 1, :] = m
        suf_stat[1, h : h + 1, :] = jnp.sum(p, axis=0, keepdims=True)
        val_t = sv_ref[:, cols].astype(F32).T.astype(BF16)
        suf_acc[cols, :] = jnp.dot(val_t, p.astype(BF16), preferred_element_type=F32)

    pltpu.make_async_copy(kbuf, kbuf, recv_sem.at[1]).wait()
    pltpu.make_async_copy(vbuf, vbuf, recv_sem.at[2]).wait()
    vt[...] = vbuf[...].astype(F32).T.astype(BF16)
    pltpu.make_async_copy(qbuf, qbuf, recv_sem.at[0]).wait()

    def prefix(r, c):
        s = lax.dot_general(kbuf[...], qbuf[r], NT, preferred_element_type=F32) * scale
        m = jnp.max(s, axis=0, keepdims=True)
        p = jnp.exp(s - m)
        total = jnp.sum(p, axis=0, keepdims=True)
        acc = jnp.dot(vt[...], p.astype(BF16), preferred_element_type=F32)
        osend[r] = (acc / total).astype(BF16)
        stsend[r] = jnp.concatenate([m, total, jnp.zeros((6, 128), F32)], axis=0)
        return c

    lax.fori_loop(0, 16, prefix, 0)

    pltpu.make_async_copy(osend.at[head], orecv.at[head], recv_sem.at[3]).start()
    pltpu.make_async_copy(stsend.at[head], strecv.at[head], recv_sem.at[4]).start()

    def send_out(j, c):
        ty, tx = (y + j // 4) % 4, (x + j % 4) % 4
        to = {"dev": ty * 8 + zh * 4 + tx}
        pltpu.make_async_remote_copy(
            osend.at[ty * 4 + tx], orecv.at[head], send_sem.at[3], recv_sem.at[3],
            device_id=to, device_id_type=MESH,
        ).start()
        pltpu.make_async_remote_copy(
            stsend.at[ty * 4 + tx], strecv.at[head], send_sem.at[4], recv_sem.at[4],
            device_id=to, device_id_type=MESH,
        ).start()
        return c

    lax.fori_loop(1, 16, send_out, 0)
    pltpu.make_async_copy(strecv, strecv, recv_sem.at[4]).wait()
    pltpu.make_async_copy(orecv, orecv, recv_sem.at[3]).wait()

    for h in range(HEADS):
        cols = slice(h * HEAD_DIM, (h + 1) * HEAD_DIM)
        pre_m, pre_l = strecv[h, 0:1, :], strecv[h, 1:2, :]
        suf_m, suf_l = suf_stat[0, h : h + 1, :], suf_stat[1, h : h + 1, :]
        top = jnp.maximum(pre_m, suf_m)
        a = jnp.exp(pre_m - top) * pre_l
        b = jnp.exp(suf_m - top)
        mixed = (orecv[h].astype(F32) * a + suf_acc[cols, :] * b) / (a + suf_l * b)
        hout[:, cols] = mixed.T.astype(BF16)

    ow_copy.wait()
    square = jnp.zeros((128, 1), F32)
    for n in range(4):
        cols = slice(n * 512, (n + 1) * 512)
        att = jnp.dot(hout[...], ow[:, cols], preferred_element_type=F32).astype(BF16)
        attended_ref[:, cols] = att
        res = tok_ref[:, cols].astype(F32) + att.astype(F32)
        resid[:, cols] = res
        square = square + jnp.sum(res * res, axis=1, keepdims=True)
    factor = lax.rsqrt(square * (1.0 / 2048.0) + 1e-06)
    normed_ref[...] = (resid[...] * factor * gain_ref[...]).astype(BF16)

    pltpu.make_async_copy(qbuf.at[pl.ds(0, 15)], qbuf.at[pl.ds(0, 15)], send_sem.at[0]).wait()
    pltpu.make_async_copy(kbuf.at[pl.ds(0, 992), :], kbuf.at[pl.ds(0, 992), :], send_sem.at[1]).wait()
    pltpu.make_async_copy(vbuf.at[pl.ds(0, 992), :], vbuf.at[pl.ds(0, 992), :], send_sem.at[2]).wait()
    pltpu.make_async_copy(osend.at[pl.ds(0, 15)], osend.at[pl.ds(0, 15)], send_sem.at[3]).wait()
    pltpu.make_async_copy(stsend.at[pl.ds(0, 15)], stsend.at[pl.ds(0, 15)], send_sem.at[4]).wait()


def attention(q, k, v, sk, sv, tok, gain, ow):
    vmem = pl.BlockSpec(memory_space=pltpu.VMEM)
    return pl.pallas_call(
        attention_kernel,
        out_shape=(jax.ShapeDtypeStruct((128, 2048), BF16), jax.ShapeDtypeStruct((128, 2048), BF16)),
        in_specs=[vmem] * 7 + [pl.BlockSpec(memory_space=pl.ANY)],
        out_specs=(vmem, vmem),
        scratch_shapes=[
            pltpu.VMEM((16, 128, 128), BF16),
            pltpu.VMEM((1024, 128), BF16),
            pltpu.VMEM((1024, 128), BF16),
            pltpu.VMEM((16, 128, 128), BF16),
            pltpu.VMEM((16, 128, 128), BF16),
            pltpu.VMEM((16, 8, 128), F32),
            pltpu.VMEM((16, 8, 128), F32),
            pltpu.VMEM((2048, 128), F32),
            pltpu.VMEM((2, 16, 128), F32),
            pltpu.VMEM((128, 1024), BF16),
            pltpu.VMEM((128, 2048), BF16),
            pltpu.VMEM((128, 2048), F32),
            pltpu.VMEM((2048, 2048), BF16),
            pltpu.SemaphoreType.DMA((5,)),
            pltpu.SemaphoreType.DMA((5,)),
            pltpu.SemaphoreType.DMA,
        ],
        compiler_params=pltpu.CompilerParams(
            collective_id=0, has_side_effects=True, vmem_limit_bytes=48 * 1024 * 1024
        ),
        name="attention",
    )(q, k, v, sk, sv, tok, gain, ow)


def half_expert(rows, gate_up, down_proj):
    hidden_units = down_proj.shape[0]
    projected = jnp.dot(rows, gate_up, preferred_element_type=F32)
    active = (jax.nn.silu(projected[:, :hidden_units]) * projected[:, hidden_units:]).astype(BF16)
    return jnp.dot(active, down_proj, preferred_element_type=F32).astype(BF16)


def on_device(
    tokens, queries, suffix_keys, suffix_values, prefix_keys, prefix_values,
    out_weight, norm_gain, routes, route_weights, gate_up_weight, down_weight,
):
    rows_here, width = tokens.shape
    experts, capacity = 64, 16
    named = routes.T[:, None, :] == jnp.arange(experts, dtype=jnp.int32)[None, :, None]
    member = jnp.sum(named.astype(F32), axis=0)
    gate = jnp.sum(jnp.where(named, route_weights.T[:, None, :], 0.0), axis=0)
    before = (jnp.arange(rows_here)[:, None] < jnp.arange(rows_here)[None, :]).astype(BF16)
    rank = jnp.dot(member.astype(BF16), before, preferred_element_type=F32)
    position = jnp.where(member > 0, rank, -1.0)
    place = position[:, None, :] == jnp.arange(capacity, dtype=F32)[None, :, None]
    selected = place.astype(BF16).reshape(experts * capacity, rows_here)
    weights = jnp.where(place, gate[:, None, :], 0.0)
    high = weights.astype(BF16)
    low = (weights - high.astype(F32)).astype(BF16)
    both = jnp.stack([high, low])[:, :, None]
    both = jnp.broadcast_to(both, (2, experts, 2, capacity, rows_here)).reshape(2, 2 * experts * capacity, rows_here)

    attended, normed = attention(
        queries, prefix_keys[0], prefix_values[0], suffix_keys, suffix_values, tokens,
        norm_gain.reshape(1, width), out_weight,
    )
    outgoing = jnp.dot(selected, normed, preferred_element_type=F32).astype(BF16)
    buffer = jnp.broadcast_to(
        outgoing.reshape(experts, 1, capacity, width), (experts, 2, capacity, width)
    ).reshape(2 * experts, capacity, width)
    received = lax.all_to_all(buffer, ("grp", "dev"), split_axis=0, concat_axis=0, tiled=True)
    partial_rows = half_expert(
        received.reshape(-1, width), gate_up_weight[0], down_weight[0]
    ).reshape(2 * experts, capacity, width)
    returned = lax.all_to_all(partial_rows, ("grp", "dev"), split_axis=0, concat_axis=0, tiled=True)
    flat = returned.reshape(-1, width)
    contract = (((0,), (0,)), ((), ()))
    routed = lax.dot_general(both[0], flat, contract, preferred_element_type=F32) + lax.dot_general(
        both[1], flat, contract, preferred_element_type=F32
    )
    return (attended, routed.astype(BF16))


def solution(mesh):
    row = P(("grp", "dev"), None)
    cube = P(("grp", "dev"), None, None)
    return jax.shard_map(
        on_device,
        mesh=mesh,
        in_specs=(row, row, row, row, P("grp", "dev", None), P("grp", "dev", None), P(), P(), row, row, cube, cube),
        out_specs=(row, row),
        check_vma=False,
    )
```

```python
import functools
import math

import jax
import jax.numpy as jnp
from jax import lax
from jax.experimental import pallas as pl
from jax.experimental.pallas import tpu as pltpu
from jax.sharding import PartitionSpec as P

HEADS = 16
HEAD_DIM = 128
TOP = 6
MESH = pl.DeviceIdType.MESH
F32 = jnp.float32
BF16 = jnp.bfloat16
NT = (((1,), (1,)), ((), ()))


def attention_kernel(
    q_ref, k_ref, v_ref, sk_ref, sv_ref, tok_ref, gain_ref, ow_hbm,
    attended_ref, normed_ref,
    qbuf, kbuf, vbuf, osend, orecv, stsend, strecv, suf_acc, suf_stat, vt, hout, resid, ow,
    recv_sem, send_sem, ow_sem,
):
    me = lax.axis_index("dev")
    y, zh, x = me // 8, (me // 4) % 2, me % 4
    head = y * 4 + x
    scale = 1.0 / math.sqrt(HEAD_DIM)

    ow_copy = pltpu.make_async_copy(ow_hbm, ow, ow_sem)
    ow_copy.start()

    barrier = pltpu.get_barrier_semaphore()

    def greet(j, c):
        pl.semaphore_signal(barrier, inc=1, device_id={"dev": (me + j) % 32}, device_id_type=MESH)
        return c

    lax.fori_loop(1, 32, greet, 0)
    pl.semaphore_wait(barrier, 31)

    def columns(h):
        return pl.ds(pl.multiple_of(h * HEAD_DIM, HEAD_DIM), HEAD_DIM)

    def key_rows(d):
        return pl.ds(pl.multiple_of(d * 32, 32), 32)

    pltpu.make_async_copy(q_ref.at[:, columns(head)], qbuf.at[head], recv_sem.at[0]).start()
    pltpu.make_async_copy(k_ref.at[:, columns(head)], kbuf.at[key_rows(me), :], recv_sem.at[1]).start()
    pltpu.make_async_copy(v_ref.at[:, columns(head)], vbuf.at[key_rows(me), :], recv_sem.at[2]).start()

    def send_kv(j, c):
        dz, dy, dx = j // 16, (j // 4) % 4, j % 4
        ty, tz, tx = (y + dy) % 4, (zh + dz) % 2, (x + dx) % 4
        to = {"dev": ty * 8 + tz * 4 + tx}
        h = ty * 4 + tx
        pltpu.make_async_remote_copy(
            k_ref.at[:, columns(h)], kbuf.at[key_rows(me), :], send_sem.at[1], recv_sem.at[1],
            device_id=to, device_id_type=MESH,
        ).start()
        pltpu.make_async_remote_copy(
            v_ref.at[:, columns(h)], vbuf.at[key_rows(me), :], send_sem.at[2], recv_sem.at[2],
            device_id=to, device_id_type=MESH,
        ).start()
        return c

    def send_q(j, c):
        ty, tx = (y + j // 4) % 4, (x + j % 4) % 4
        h = ty * 4 + tx
        pltpu.make_async_remote_copy(
            q_ref.at[:, columns(h)], qbuf.at[head], send_sem.at[0], recv_sem.at[0],
            device_id={"dev": ty * 8 + zh * 4 + tx}, device_id_type=MESH,
        ).start()
        return c

    lax.fori_loop(1, 32, send_kv, 0)
    lax.fori_loop(1, 16, send_q, 0)

    key_at = lax.broadcasted_iota(jnp.int32, (128, 128), 0)
    query_at = lax.broadcasted_iota(jnp.int32, (128, 128), 1)
    allowed = key_at <= query_at
    for h in range(HEADS):
        cols = slice(h * HEAD_DIM, (h + 1) * HEAD_DIM)
        s = lax.dot_general(sk_ref[:, cols], q_ref[:, cols], NT, preferred_element_type=F32) * scale
        s = jnp.where(allowed, s, -jnp.inf)
        m = jnp.max(s, axis=0, keepdims=True)
        p = jnp.exp(s - m)
        suf_stat[0, h : h + 1, :] = m
        suf_stat[1, h : h + 1, :] = jnp.sum(p, axis=0, keepdims=True)
        val_t = sv_ref[:, cols].astype(F32).T.astype(BF16)
        suf_acc[cols, :] = jnp.dot(val_t, p.astype(BF16), preferred_element_type=F32)

    pltpu.make_async_copy(kbuf, kbuf, recv_sem.at[1]).wait()
    pltpu.make_async_copy(vbuf, vbuf, recv_sem.at[2]).wait()
    vt[...] = vbuf[...].astype(F32).T.astype(BF16)
    pltpu.make_async_copy(qbuf, qbuf, recv_sem.at[0]).wait()

    def prefix(r, c):
        s = lax.dot_general(kbuf[...], qbuf[r], NT, preferred_element_type=F32) * scale
        m = jnp.max(s, axis=0, keepdims=True)
        p = jnp.exp(s - m)
        total = jnp.sum(p, axis=0, keepdims=True)
        acc = jnp.dot(vt[...], p.astype(BF16), preferred_element_type=F32)
        osend[r] = (acc / total).astype(BF16)
        stsend[r] = jnp.concatenate([m, total, jnp.zeros((6, 128), F32)], axis=0)
        return c

    lax.fori_loop(0, 16, prefix, 0)

    pltpu.make_async_copy(osend.at[head], orecv.at[head], recv_sem.at[3]).start()
    pltpu.make_async_copy(stsend.at[head], strecv.at[head], recv_sem.at[4]).start()

    def send_out(j, c):
        ty, tx = (y + j // 4) % 4, (x + j % 4) % 4
        to = {"dev": ty * 8 + zh * 4 + tx}
        pltpu.make_async_remote_copy(
            osend.at[ty * 4 + tx], orecv.at[head], send_sem.at[3], recv_sem.at[3],
            device_id=to, device_id_type=MESH,
        ).start()
        pltpu.make_async_remote_copy(
            stsend.at[ty * 4 + tx], strecv.at[head], send_sem.at[4], recv_sem.at[4],
            device_id=to, device_id_type=MESH,
        ).start()
        return c

    lax.fori_loop(1, 16, send_out, 0)
    pltpu.make_async_copy(strecv, strecv, recv_sem.at[4]).wait()
    pltpu.make_async_copy(orecv, orecv, recv_sem.at[3]).wait()

    for h in range(HEADS):
        cols = slice(h * HEAD_DIM, (h + 1) * HEAD_DIM)
        pre_m, pre_l = strecv[h, 0:1, :], strecv[h, 1:2, :]
        suf_m, suf_l = suf_stat[0, h : h + 1, :], suf_stat[1, h : h + 1, :]
        top = jnp.maximum(pre_m, suf_m)
        a = jnp.exp(pre_m - top) * pre_l
        b = jnp.exp(suf_m - top)
        mixed = (orecv[h].astype(F32) * a + suf_acc[cols, :] * b) / (a + suf_l * b)
        hout[:, cols] = mixed.T.astype(BF16)

    ow_copy.wait()
    square = jnp.zeros((128, 1), F32)
    for n in range(4):
        cols = slice(n * 512, (n + 1) * 512)
        att = jnp.dot(hout[...], ow[:, cols], preferred_element_type=F32).astype(BF16)
        attended_ref[:, cols] = att
        res = tok_ref[:, cols].astype(F32) + att.astype(F32)
        resid[:, cols] = res
        square = square + jnp.sum(res * res, axis=1, keepdims=True)
    factor = lax.rsqrt(square * (1.0 / 2048.0) + 1e-06)
    normed_ref[...] = (resid[...] * factor * gain_ref[...]).astype(BF16)

    pltpu.make_async_copy(qbuf.at[pl.ds(0, 15)], qbuf.at[pl.ds(0, 15)], send_sem.at[0]).wait()
    pltpu.make_async_copy(kbuf.at[pl.ds(0, 992), :], kbuf.at[pl.ds(0, 992), :], send_sem.at[1]).wait()
    pltpu.make_async_copy(vbuf.at[pl.ds(0, 992), :], vbuf.at[pl.ds(0, 992), :], send_sem.at[2]).wait()
    pltpu.make_async_copy(osend.at[pl.ds(0, 15)], osend.at[pl.ds(0, 15)], send_sem.at[3]).wait()
    pltpu.make_async_copy(stsend.at[pl.ds(0, 15)], stsend.at[pl.ds(0, 15)], send_sem.at[4]).wait()


def attention(q, k, v, sk, sv, tok, gain, ow):
    vmem = pl.BlockSpec(memory_space=pltpu.VMEM)
    return pl.pallas_call(
        attention_kernel,
        out_shape=(jax.ShapeDtypeStruct((128, 2048), BF16), jax.ShapeDtypeStruct((128, 2048), BF16)),
        in_specs=[vmem] * 7 + [pl.BlockSpec(memory_space=pl.ANY)],
        out_specs=(vmem, vmem),
        scratch_shapes=[
            pltpu.VMEM((16, 128, 128), BF16),
            pltpu.VMEM((1024, 128), BF16),
            pltpu.VMEM((1024, 128), BF16),
            pltpu.VMEM((16, 128, 128), BF16),
            pltpu.VMEM((16, 128, 128), BF16),
            pltpu.VMEM((16, 8, 128), F32),
            pltpu.VMEM((16, 8, 128), F32),
            pltpu.VMEM((2048, 128), F32),
            pltpu.VMEM((2, 16, 128), F32),
            pltpu.VMEM((128, 1024), BF16),
            pltpu.VMEM((128, 2048), BF16),
            pltpu.VMEM((128, 2048), F32),
            pltpu.VMEM((2048, 2048), BF16),
            pltpu.SemaphoreType.DMA((5,)),
            pltpu.SemaphoreType.DMA((5,)),
            pltpu.SemaphoreType.DMA,
        ],
        compiler_params=pltpu.CompilerParams(
            collective_id=0, has_side_effects=True, vmem_limit_bytes=48 * 1024 * 1024
        ),
        name="attention",
    )(q, k, v, sk, sv, tok, gain, ow)


def activation(rows, gate_up):
    hidden_units = gate_up.shape[1] // 2
    projected = jnp.dot(rows, gate_up, preferred_element_type=F32)
    return (jax.nn.silu(projected[:, :hidden_units]) * projected[:, hidden_units:]).astype(BF16)


AXES = ("grp", "dev")
SWAP = [(i, i ^ 1) for i in range(128)]
SERVED = [[i for i in range(128) if i % 4 in xs] for xs in ((0, 3), (1, 2))]


def on_device(
    tokens, queries, suffix_keys, suffix_values, prefix_keys, prefix_values,
    out_weight, norm_gain, routes, route_weights, gate_up_weight, down_weight,
):
    rows_here, width = tokens.shape
    experts, capacity = 64, 16
    own_down = down_weight[0]
    partner_down = lax.ppermute(own_down, AXES, SWAP)
    named = routes.T[:, None, :] == jnp.arange(experts, dtype=jnp.int32)[None, :, None]
    member = jnp.sum(named.astype(F32), axis=0)
    gate = jnp.sum(jnp.where(named, route_weights.T[:, None, :], 0.0), axis=0)
    before = (jnp.arange(rows_here)[:, None] < jnp.arange(rows_here)[None, :]).astype(BF16)
    rank = jnp.dot(member.astype(BF16), before, preferred_element_type=F32)
    position = jnp.where(member > 0, rank, -1.0)
    slot = jnp.arange(capacity, dtype=F32)
    twice = jnp.broadcast_to(position[:, None, :], (experts, 2, rows_here))
    selected = (twice[:, :, None, :] == slot[None, None, :, None]).astype(BF16)
    selected = selected.reshape(2 * experts * capacity, rows_here)
    weights = jnp.where(position[:, None, :] == slot[None, :, None], gate[:, None, :], 0.0)
    weights = weights.reshape(experts * capacity, rows_here)
    high = weights.astype(BF16)
    low = (weights - high.astype(F32)).astype(BF16)
    both = jnp.concatenate([high, low], axis=1)

    attended, normed = attention(
        queries, prefix_keys[0], prefix_values[0], suffix_keys, suffix_values, tokens,
        norm_gain.reshape(1, width), out_weight,
    )
    outgoing = jnp.dot(selected, normed, preferred_element_type=F32).astype(BF16)
    received = lax.all_to_all(
        outgoing.reshape(2 * experts, capacity, width), AXES, split_axis=0, concat_axis=0, tiled=True
    )
    by_x = received.reshape(experts // 2, 4, capacity, width)
    x = lax.axis_index("dev") % 4
    outer = (x % 3 == 0).astype(jnp.int32)
    mine = (1 - outer, 2 + outer)
    others = (outer, 3 - outer)

    def act_of(at):
        rows = lax.dynamic_index_in_dim(by_x, at, axis=1, keepdims=False)
        return activation(rows.reshape(-1, width), gate_up_weight[0])

    swapped = []
    for at in others:
        swapped.append(lax.ppermute(act_of(at), AXES, SWAP))
    kept = [act_of(at) for at in mine]
    finished = [
        (
            jnp.dot(k, own_down, preferred_element_type=F32)
            + jnp.dot(s, partner_down, preferred_element_type=F32)
        ).astype(BF16).reshape(experts // 2, 1, capacity, width)
        for k, s in zip(kept, swapped)
    ]
    partial_rows = jnp.concatenate(finished, axis=1).reshape(experts, capacity, width)
    returned = lax.all_to_all(
        partial_rows, AXES, split_axis=0, concat_axis=0, axis_index_groups=SERVED, tiled=True
    )
    flat = returned.reshape(-1, width)
    parts = lax.dot_general(both, flat, (((0,), (0,)), ((), ())), preferred_element_type=F32)
    routed = parts[:rows_here] + parts[rows_here:]
    return (attended, routed.astype(BF16))


def solution(mesh):
    row = P(("grp", "dev"), None)
    cube = P(("grp", "dev"), None, None)
    return jax.shard_map(
        on_device,
        mesh=mesh,
        in_specs=(row, row, row, row, P("grp", "dev", None), P("grp", "dev", None), P(), P(), row, row, cube, cube),
        out_specs=(row, row),
        check_vma=False,
    )
```

```python
import functools
import math

import jax
import jax.numpy as jnp
from jax import lax
from jax.experimental import pallas as pl
from jax.experimental.pallas import tpu as pltpu
from jax.sharding import PartitionSpec as P

HEADS = 16
HEAD_DIM = 128
TOP = 6
MESH = pl.DeviceIdType.MESH
F32 = jnp.float32
BF16 = jnp.bfloat16
NT = (((1,), (1,)), ((), ()))


def attention_kernel(
    q_ref, k_ref, v_ref, sk_ref, sv_ref, tok_ref, gain_ref, ow_hbm,
    attended_ref, normed_ref,
    qbuf, kbuf, vbuf, osend, orecv, stsend, strecv, suf_acc, suf_stat, vt, hout, resid, ow,
    recv_sem, send_sem, ow_sem,
):
    me = lax.axis_index("dev")
    y, zh, x = me // 8, (me // 4) % 2, me % 4
    head = y * 4 + x
    scale = 1.0 / math.sqrt(HEAD_DIM)

    ow_copy = pltpu.make_async_copy(ow_hbm, ow, ow_sem)
    ow_copy.start()

    barrier = pltpu.get_barrier_semaphore()

    def greet(j, c):
        pl.semaphore_signal(barrier, inc=1, device_id={"dev": (me + j) % 32}, device_id_type=MESH)
        return c

    lax.fori_loop(1, 32, greet, 0)
    pl.semaphore_wait(barrier, 31)

    def columns(h):
        return pl.ds(pl.multiple_of(h * HEAD_DIM, HEAD_DIM), HEAD_DIM)

    def key_rows(d):
        return pl.ds(pl.multiple_of(d * 32, 32), 32)

    pltpu.make_async_copy(q_ref.at[:, columns(head)], qbuf.at[head], recv_sem.at[0]).start()
    pltpu.make_async_copy(k_ref.at[:, columns(head)], kbuf.at[key_rows(me), :], recv_sem.at[1]).start()
    pltpu.make_async_copy(v_ref.at[:, columns(head)], vbuf.at[key_rows(me), :], recv_sem.at[2]).start()

    def send_kv(j, c):
        dz, dy, dx = j // 16, (j // 4) % 4, j % 4
        ty, tz, tx = (y + dy) % 4, (zh + dz) % 2, (x + dx) % 4
        to = {"dev": ty * 8 + tz * 4 + tx}
        h = ty * 4 + tx
        pltpu.make_async_remote_copy(
            k_ref.at[:, columns(h)], kbuf.at[key_rows(me), :], send_sem.at[1], recv_sem.at[1],
            device_id=to, device_id_type=MESH,
        ).start()
        pltpu.make_async_remote_copy(
            v_ref.at[:, columns(h)], vbuf.at[key_rows(me), :], send_sem.at[2], recv_sem.at[2],
            device_id=to, device_id_type=MESH,
        ).start()
        return c

    def send_q(j, c):
        ty, tx = (y + j // 4) % 4, (x + j % 4) % 4
        h = ty * 4 + tx
        pltpu.make_async_remote_copy(
            q_ref.at[:, columns(h)], qbuf.at[head], send_sem.at[0], recv_sem.at[0],
            device_id={"dev": ty * 8 + zh * 4 + tx}, device_id_type=MESH,
        ).start()
        return c

    lax.fori_loop(1, 32, send_kv, 0)
    lax.fori_loop(1, 16, send_q, 0)

    key_at = lax.broadcasted_iota(jnp.int32, (128, 128), 0)
    query_at = lax.broadcasted_iota(jnp.int32, (128, 128), 1)
    allowed = key_at <= query_at
    for h in range(HEADS):
        cols = slice(h * HEAD_DIM, (h + 1) * HEAD_DIM)
        s = lax.dot_general(sk_ref[:, cols], q_ref[:, cols], NT, preferred_element_type=F32) * scale
        s = jnp.where(allowed, s, -jnp.inf)
        m = jnp.max(s, axis=0, keepdims=True)
        p = jnp.exp(s - m)
        suf_stat[0, h : h + 1, :] = m
        suf_stat[1, h : h + 1, :] = jnp.sum(p, axis=0, keepdims=True)
        val_t = sv_ref[:, cols].astype(F32).T.astype(BF16)
        suf_acc[cols, :] = jnp.dot(val_t, p.astype(BF16), preferred_element_type=F32)

    pltpu.make_async_copy(kbuf, kbuf, recv_sem.at[1]).wait()
    pltpu.make_async_copy(vbuf, vbuf, recv_sem.at[2]).wait()
    vt[...] = vbuf[...].astype(F32).T.astype(BF16)
    pltpu.make_async_copy(qbuf, qbuf, recv_sem.at[0]).wait()

    def prefix(r, c):
        s = lax.dot_general(kbuf[...], qbuf[r], NT, preferred_element_type=F32) * scale
        m = jnp.max(s, axis=0, keepdims=True)
        p = jnp.exp(s - m)
        total = jnp.sum(p, axis=0, keepdims=True)
        acc = jnp.dot(vt[...], p.astype(BF16), preferred_element_type=F32)
        osend[r] = (acc / total).astype(BF16)
        stsend[r] = jnp.concatenate([m, total, jnp.zeros((6, 128), F32)], axis=0)
        return c

    lax.fori_loop(0, 16, prefix, 0)

    pltpu.make_async_copy(osend.at[head], orecv.at[head], recv_sem.at[3]).start()
    pltpu.make_async_copy(stsend.at[head], strecv.at[head], recv_sem.at[4]).start()

    def send_out(j, c):
        ty, tx = (y + j // 4) % 4, (x + j % 4) % 4
        to = {"dev": ty * 8 + zh * 4 + tx}
        pltpu.make_async_remote_copy(
            osend.at[ty * 4 + tx], orecv.at[head], send_sem.at[3], recv_sem.at[3],
            device_id=to, device_id_type=MESH,
        ).start()
        pltpu.make_async_remote_copy(
            stsend.at[ty * 4 + tx], strecv.at[head], send_sem.at[4], recv_sem.at[4],
            device_id=to, device_id_type=MESH,
        ).start()
        return c

    lax.fori_loop(1, 16, send_out, 0)
    pltpu.make_async_copy(strecv, strecv, recv_sem.at[4]).wait()
    pltpu.make_async_copy(orecv, orecv, recv_sem.at[3]).wait()

    for h in range(HEADS):
        cols = slice(h * HEAD_DIM, (h + 1) * HEAD_DIM)
        pre_m, pre_l = strecv[h, 0:1, :], strecv[h, 1:2, :]
        suf_m, suf_l = suf_stat[0, h : h + 1, :], suf_stat[1, h : h + 1, :]
        top = jnp.maximum(pre_m, suf_m)
        a = jnp.exp(pre_m - top) * pre_l
        b = jnp.exp(suf_m - top)
        mixed = (orecv[h].astype(F32) * a + suf_acc[cols, :] * b) / (a + suf_l * b)
        hout[:, cols] = mixed.T.astype(BF16)

    ow_copy.wait()
    square = jnp.zeros((128, 1), F32)
    for n in range(4):
        cols = slice(n * 512, (n + 1) * 512)
        att = jnp.dot(hout[...], ow[:, cols], preferred_element_type=F32).astype(BF16)
        attended_ref[:, cols] = att
        res = tok_ref[:, cols].astype(F32) + att.astype(F32)
        resid[:, cols] = res
        square = square + jnp.sum(res * res, axis=1, keepdims=True)
    factor = lax.rsqrt(square * (1.0 / 2048.0) + 1e-06)
    normed_ref[...] = (resid[...] * factor * gain_ref[...]).astype(BF16)

    pltpu.make_async_copy(qbuf.at[pl.ds(0, 15)], qbuf.at[pl.ds(0, 15)], send_sem.at[0]).wait()
    pltpu.make_async_copy(kbuf.at[pl.ds(0, 992), :], kbuf.at[pl.ds(0, 992), :], send_sem.at[1]).wait()
    pltpu.make_async_copy(vbuf.at[pl.ds(0, 992), :], vbuf.at[pl.ds(0, 992), :], send_sem.at[2]).wait()
    pltpu.make_async_copy(osend.at[pl.ds(0, 15)], osend.at[pl.ds(0, 15)], send_sem.at[3]).wait()
    pltpu.make_async_copy(stsend.at[pl.ds(0, 15)], stsend.at[pl.ds(0, 15)], send_sem.at[4]).wait()


def attention(q, k, v, sk, sv, tok, gain, ow):
    vmem = pl.BlockSpec(memory_space=pltpu.VMEM)
    return pl.pallas_call(
        attention_kernel,
        out_shape=(jax.ShapeDtypeStruct((128, 2048), BF16), jax.ShapeDtypeStruct((128, 2048), BF16)),
        in_specs=[vmem] * 7 + [pl.BlockSpec(memory_space=pl.ANY)],
        out_specs=(vmem, vmem),
        scratch_shapes=[
            pltpu.VMEM((16, 128, 128), BF16),
            pltpu.VMEM((1024, 128), BF16),
            pltpu.VMEM((1024, 128), BF16),
            pltpu.VMEM((16, 128, 128), BF16),
            pltpu.VMEM((16, 128, 128), BF16),
            pltpu.VMEM((16, 8, 128), F32),
            pltpu.VMEM((16, 8, 128), F32),
            pltpu.VMEM((2048, 128), F32),
            pltpu.VMEM((2, 16, 128), F32),
            pltpu.VMEM((128, 1024), BF16),
            pltpu.VMEM((128, 2048), BF16),
            pltpu.VMEM((128, 2048), F32),
            pltpu.VMEM((2048, 2048), BF16),
            pltpu.SemaphoreType.DMA((5,)),
            pltpu.SemaphoreType.DMA((5,)),
            pltpu.SemaphoreType.DMA,
        ],
        compiler_params=pltpu.CompilerParams(
            collective_id=0, has_side_effects=True, vmem_limit_bytes=48 * 1024 * 1024
        ),
        name="attention",
    )(q, k, v, sk, sv, tok, gain, ow)


def half_expert(rows, gate_up, down_proj):
    hidden_units = down_proj.shape[0]
    projected = jnp.dot(rows, gate_up, preferred_element_type=F32)
    active = (jax.nn.silu(projected[:, :hidden_units]) * projected[:, hidden_units:]).astype(BF16)
    return jnp.dot(active, down_proj, preferred_element_type=F32).astype(BF16)


AXES = ("grp", "dev")
CHUNKS = 2


def on_device(
    tokens, queries, suffix_keys, suffix_values, prefix_keys, prefix_values,
    out_weight, norm_gain, routes, route_weights, gate_up_weight, down_weight,
):
    rows_here, width = tokens.shape
    experts, capacity = 64, 16
    depth = capacity // CHUNKS
    named = routes.T[:, None, :] == jnp.arange(experts, dtype=jnp.int32)[None, :, None]
    member = jnp.sum(named.astype(F32), axis=0)
    gate = jnp.sum(jnp.where(named, route_weights.T[:, None, :], 0.0), axis=0)
    before = (jnp.arange(rows_here)[:, None] < jnp.arange(rows_here)[None, :]).astype(BF16)
    rank = jnp.dot(member.astype(BF16), before, preferred_element_type=F32)
    position = jnp.where(member > 0, rank, -1.0)

    def both_halves(a):
        shape = (experts, 2, depth, rows_here)
        return jnp.broadcast_to(a.reshape(experts, 1, 1, rows_here), shape)

    attended, normed = attention(
        queries, prefix_keys[0], prefix_values[0], suffix_keys, suffix_values, tokens,
        norm_gain.reshape(1, width), out_weight,
    )

    def exchange(rows):
        return lax.all_to_all(
            rows.reshape(2 * experts, depth, width), AXES, split_axis=0, concat_axis=0, tiled=True
        ).reshape(2 * experts * depth, width)

    places, received = [], []
    for n in range(CHUNKS):
        slot = jnp.arange(n * depth, (n + 1) * depth, dtype=F32)[None, None, :, None]
        place = both_halves(position) == slot
        places.append(place)
        selected = place.astype(BF16).reshape(2 * experts * depth, rows_here)
        received.append(exchange(jnp.dot(selected, normed, preferred_element_type=F32).astype(BF16)))
    returned = [exchange(half_expert(rows, gate_up_weight[0], down_weight[0])) for rows in received]
    total = jnp.zeros((2 * rows_here, width), F32)
    for place, rows in zip(places, returned):
        weights = jnp.where(place, both_halves(gate), 0.0).reshape(2 * experts * depth, rows_here)
        high = weights.astype(BF16)
        low = (weights - high.astype(F32)).astype(BF16)
        both = jnp.concatenate([high, low], axis=1)
        total = total + lax.dot_general(both, rows, (((0,), (0,)), ((), ())), preferred_element_type=F32)
    return (attended, (total[:rows_here] + total[rows_here:]).astype(BF16))


def solution(mesh):
    row = P(("grp", "dev"), None)
    cube = P(("grp", "dev"), None, None)
    return jax.shard_map(
        on_device,
        mesh=mesh,
        in_specs=(row, row, row, row, P("grp", "dev", None), P("grp", "dev", None), P(), P(), row, row, cube, cube),
        out_specs=(row, row),
        check_vma=False,
    )
```

```python
import functools
import math

import jax
import jax.numpy as jnp
from jax import lax
from jax.experimental import pallas as pl
from jax.experimental.pallas import tpu as pltpu
from jax.sharding import PartitionSpec as P

HEADS = 16
HEAD_DIM = 128
TOP = 6
MESH = pl.DeviceIdType.MESH
F32 = jnp.float32
BF16 = jnp.bfloat16
NT = (((1,), (1,)), ((), ()))


def attention_kernel(
    q_ref, k_ref, v_ref, sk_ref, sv_ref, tok_ref, gain_ref, ow_hbm,
    attended_ref, normed_ref,
    qbuf, kbuf, vbuf, osend, orecv, stsend, strecv, suf_acc, suf_stat, vt, hout, resid, ow,
    recv_sem, send_sem, ow_sem,
):
    me = lax.axis_index("dev")
    y, zh, x = me // 8, (me // 4) % 2, me % 4
    head = y * 4 + x
    scale = 1.0 / math.sqrt(HEAD_DIM)

    ow_copy = pltpu.make_async_copy(ow_hbm, ow, ow_sem)
    ow_copy.start()

    barrier = pltpu.get_barrier_semaphore()

    def greet(j, c):
        pl.semaphore_signal(barrier, inc=1, device_id={"dev": (me + j) % 32}, device_id_type=MESH)
        return c

    lax.fori_loop(1, 32, greet, 0)
    pl.semaphore_wait(barrier, 31)

    def columns(h):
        return pl.ds(pl.multiple_of(h * HEAD_DIM, HEAD_DIM), HEAD_DIM)

    def key_rows(d):
        return pl.ds(pl.multiple_of(d * 32, 32), 32)

    pltpu.make_async_copy(q_ref.at[:, columns(head)], qbuf.at[head], recv_sem.at[0]).start()
    pltpu.make_async_copy(k_ref.at[:, columns(head)], kbuf.at[key_rows(me), :], recv_sem.at[1]).start()
    pltpu.make_async_copy(v_ref.at[:, columns(head)], vbuf.at[key_rows(me), :], recv_sem.at[2]).start()

    def send_kv(j, c):
        dz, dy, dx = j // 16, (j // 4) % 4, j % 4
        ty, tz, tx = (y + dy) % 4, (zh + dz) % 2, (x + dx) % 4
        to = {"dev": ty * 8 + tz * 4 + tx}
        h = ty * 4 + tx
        pltpu.make_async_remote_copy(
            k_ref.at[:, columns(h)], kbuf.at[key_rows(me), :], send_sem.at[1], recv_sem.at[1],
            device_id=to, device_id_type=MESH,
        ).start()
        pltpu.make_async_remote_copy(
            v_ref.at[:, columns(h)], vbuf.at[key_rows(me), :], send_sem.at[2], recv_sem.at[2],
            device_id=to, device_id_type=MESH,
        ).start()
        return c

    def send_q(j, c):
        ty, tx = (y + j // 4) % 4, (x + j % 4) % 4
        h = ty * 4 + tx
        pltpu.make_async_remote_copy(
            q_ref.at[:, columns(h)], qbuf.at[head], send_sem.at[0], recv_sem.at[0],
            device_id={"dev": ty * 8 + zh * 4 + tx}, device_id_type=MESH,
        ).start()
        return c

    lax.fori_loop(1, 32, send_kv, 0)
    lax.fori_loop(1, 16, send_q, 0)

    key_at = lax.broadcasted_iota(jnp.int32, (128, 128), 0)
    query_at = lax.broadcasted_iota(jnp.int32, (128, 128), 1)
    allowed = key_at <= query_at
    for h in range(HEADS):
        cols = slice(h * HEAD_DIM, (h + 1) * HEAD_DIM)
        s = lax.dot_general(sk_ref[:, cols], q_ref[:, cols], NT, preferred_element_type=F32) * scale
        s = jnp.where(allowed, s, -jnp.inf)
        m = jnp.max(s, axis=0, keepdims=True)
        p = jnp.exp(s - m)
        suf_stat[0, h : h + 1, :] = m
        suf_stat[1, h : h + 1, :] = jnp.sum(p, axis=0, keepdims=True)
        val_t = sv_ref[:, cols].astype(F32).T.astype(BF16)
        suf_acc[cols, :] = jnp.dot(val_t, p.astype(BF16), preferred_element_type=F32)

    pltpu.make_async_copy(kbuf, kbuf, recv_sem.at[1]).wait()
    pltpu.make_async_copy(vbuf, vbuf, recv_sem.at[2]).wait()
    vt[...] = vbuf[...].astype(F32).T.astype(BF16)
    pltpu.make_async_copy(qbuf, qbuf, recv_sem.at[0]).wait()

    def prefix(r, c):
        s = lax.dot_general(kbuf[...], qbuf[r], NT, preferred_element_type=F32) * scale
        m = jnp.max(s, axis=0, keepdims=True)
        p = jnp.exp(s - m)
        total = jnp.sum(p, axis=0, keepdims=True)
        acc = jnp.dot(vt[...], p.astype(BF16), preferred_element_type=F32)
        osend[r] = (acc / total).astype(BF16)
        stsend[r] = jnp.concatenate([m, total, jnp.zeros((6, 128), F32)], axis=0)
        return c

    lax.fori_loop(0, 16, prefix, 0)

    pltpu.make_async_copy(osend.at[head], orecv.at[head], recv_sem.at[3]).start()
    pltpu.make_async_copy(stsend.at[head], strecv.at[head], recv_sem.at[4]).start()

    def send_out(j, c):
        ty, tx = (y + j // 4) % 4, (x + j % 4) % 4
        to = {"dev": ty * 8 + zh * 4 + tx}
        pltpu.make_async_remote_copy(
            osend.at[ty * 4 + tx], orecv.at[head], send_sem.at[3], recv_sem.at[3],
            device_id=to, device_id_type=MESH,
        ).start()
        pltpu.make_async_remote_copy(
            stsend.at[ty * 4 + tx], strecv.at[head], send_sem.at[4], recv_sem.at[4],
            device_id=to, device_id_type=MESH,
        ).start()
        return c

    lax.fori_loop(1, 16, send_out, 0)
    pltpu.make_async_copy(strecv, strecv, recv_sem.at[4]).wait()
    pltpu.make_async_copy(orecv, orecv, recv_sem.at[3]).wait()

    for h in range(HEADS):
        cols = slice(h * HEAD_DIM, (h + 1) * HEAD_DIM)
        pre_m, pre_l = strecv[h, 0:1, :], strecv[h, 1:2, :]
        suf_m, suf_l = suf_stat[0, h : h + 1, :], suf_stat[1, h : h + 1, :]
        top = jnp.maximum(pre_m, suf_m)
        a = jnp.exp(pre_m - top) * pre_l
        b = jnp.exp(suf_m - top)
        mixed = (orecv[h].astype(F32) * a + suf_acc[cols, :] * b) / (a + suf_l * b)
        hout[:, cols] = mixed.T.astype(BF16)

    ow_copy.wait()
    square = jnp.zeros((128, 1), F32)
    for n in range(4):
        cols = slice(n * 512, (n + 1) * 512)
        att = jnp.dot(hout[...], ow[:, cols], preferred_element_type=F32).astype(BF16)
        attended_ref[:, cols] = att
        res = tok_ref[:, cols].astype(F32) + att.astype(F32)
        resid[:, cols] = res
        square = square + jnp.sum(res * res, axis=1, keepdims=True)
    factor = lax.rsqrt(square * (1.0 / 2048.0) + 1e-06)
    normed_ref[...] = (resid[...] * factor * gain_ref[...]).astype(BF16)

    pltpu.make_async_copy(qbuf.at[pl.ds(0, 15)], qbuf.at[pl.ds(0, 15)], send_sem.at[0]).wait()
    pltpu.make_async_copy(kbuf.at[pl.ds(0, 992), :], kbuf.at[pl.ds(0, 992), :], send_sem.at[1]).wait()
    pltpu.make_async_copy(vbuf.at[pl.ds(0, 992), :], vbuf.at[pl.ds(0, 992), :], send_sem.at[2]).wait()
    pltpu.make_async_copy(osend.at[pl.ds(0, 15)], osend.at[pl.ds(0, 15)], send_sem.at[3]).wait()
    pltpu.make_async_copy(stsend.at[pl.ds(0, 15)], stsend.at[pl.ds(0, 15)], send_sem.at[4]).wait()


def attention(q, k, v, sk, sv, tok, gain, ow):
    vmem = pl.BlockSpec(memory_space=pltpu.VMEM)
    return pl.pallas_call(
        attention_kernel,
        out_shape=(jax.ShapeDtypeStruct((128, 2048), BF16), jax.ShapeDtypeStruct((128, 2048), BF16)),
        in_specs=[vmem] * 7 + [pl.BlockSpec(memory_space=pl.ANY)],
        out_specs=(vmem, vmem),
        scratch_shapes=[
            pltpu.VMEM((16, 128, 128), BF16),
            pltpu.VMEM((1024, 128), BF16),
            pltpu.VMEM((1024, 128), BF16),
            pltpu.VMEM((16, 128, 128), BF16),
            pltpu.VMEM((16, 128, 128), BF16),
            pltpu.VMEM((16, 8, 128), F32),
            pltpu.VMEM((16, 8, 128), F32),
            pltpu.VMEM((2048, 128), F32),
            pltpu.VMEM((2, 16, 128), F32),
            pltpu.VMEM((128, 1024), BF16),
            pltpu.VMEM((128, 2048), BF16),
            pltpu.VMEM((128, 2048), F32),
            pltpu.VMEM((2048, 2048), BF16),
            pltpu.SemaphoreType.DMA((5,)),
            pltpu.SemaphoreType.DMA((5,)),
            pltpu.SemaphoreType.DMA,
        ],
        compiler_params=pltpu.CompilerParams(
            collective_id=0, has_side_effects=True, vmem_limit_bytes=48 * 1024 * 1024
        ),
        name="attention",
    )(q, k, v, sk, sv, tok, gain, ow)


def experts_kernel(
    out_ref, gu_hbm, down_hbm, flat_ref,
    recv, part, gu, down, proj, act,
    recv_sem, send_sem, weight_sem,
):
    me = lax.axis_index("grp") * 32 + lax.axis_index("dev")
    gu_copy = pltpu.make_async_copy(gu_hbm, gu, weight_sem.at[0])
    down_copy = pltpu.make_async_copy(down_hbm, down, weight_sem.at[1])
    gu_copy.start()
    down_copy.start()

    def place(i):
        return {"grp": i // 32, "dev": i % 32}

    barrier = pltpu.get_barrier_semaphore()

    def greet(j, c):
        pl.semaphore_signal(barrier, inc=1, device_id=place((me + j) % 128), device_id_type=MESH)
        return c

    lax.fori_loop(1, 128, greet, 0)
    pl.semaphore_wait(barrier, 127)

    pltpu.make_async_copy(out_ref.at[me // 2], recv.at[0], recv_sem.at[0]).start()

    def send(j, c):
        to = (me + j) % 128
        pltpu.make_async_remote_copy(
            out_ref.at[to // 2], recv.at[j], send_sem.at[0], recv_sem.at[j // 16],
            device_id=place(to), device_id_type=MESH,
        ).start()
        return c

    lax.fori_loop(1, 128, send, 0)
    gu_copy.wait()
    down_copy.wait()

    def compute(g):
        block = pl.ds(g * 16, 16)
        pltpu.make_async_copy(recv.at[block], recv.at[block], recv_sem.at[g]).wait()
        rows = recv[block].reshape(256, 2048)

        def project(n, c):
            cols = pl.ds(pl.multiple_of(n * 256, 256), 256)
            proj[:, cols] = jnp.dot(rows, gu[:, cols], preferred_element_type=F32)
            return c

        lax.fori_loop(0, 5, project, 0)
        proj[:, 1280:1408] = jnp.dot(rows, gu[:, 1280:1408], preferred_element_type=F32)
        whole = proj[...]
        up = pltpu.roll(whole, 704, 1)
        gate = whole[:, :768]
        act[...] = (gate / (1.0 + jnp.exp(-gate)) * up[:, :768]).astype(BF16)
        hidden = act[:, :704]

        def lower(n, c):
            cols = pl.ds(pl.multiple_of(n * 512, 512), 512)
            done = jnp.dot(hidden, down[:, cols], preferred_element_type=F32).astype(BF16)
            part[block, :, cols] = done.reshape(16, 16, 512)
            return c

        lax.fori_loop(0, 4, lower, 0)

    def give_back(j, c):
        pltpu.make_async_remote_copy(
            part.at[j], flat_ref.at[me], send_sem.at[1], recv_sem.at[8],
            device_id=place((me + 128 - j) % 128), device_id_type=MESH,
        ).start()
        return c

    compute(0)
    pltpu.make_async_copy(part.at[0], flat_ref.at[me], recv_sem.at[8]).start()
    lax.fori_loop(1, 16, give_back, 0)

    def group(g, c):
        compute(g)
        lax.fori_loop(g * 16, g * 16 + 16, give_back, 0)
        return c

    lax.fori_loop(1, 8, group, 0)
    sent = pl.ds(0, 127)
    pltpu.make_async_copy(recv.at[sent], recv.at[sent], send_sem.at[0]).wait()
    pltpu.make_async_copy(part.at[sent], part.at[sent], send_sem.at[1]).wait()
    pltpu.make_async_copy(flat_ref, flat_ref, recv_sem.at[8]).wait()


def expert_rows(outgoing, gate_up, down):
    vmem = pl.BlockSpec(memory_space=pltpu.VMEM)
    hbm = pl.BlockSpec(memory_space=pl.ANY)
    return pl.pallas_call(
        experts_kernel,
        out_shape=jax.ShapeDtypeStruct((128, 16, 2048), BF16),
        in_specs=[vmem, hbm, hbm],
        out_specs=vmem,
        scratch_shapes=[
            pltpu.VMEM((128, 16, 2048), BF16),
            pltpu.VMEM((128, 16, 2048), BF16),
            pltpu.VMEM((2048, 1408), BF16),
            pltpu.VMEM((704, 2048), BF16),
            pltpu.VMEM((256, 1408), F32),
            pltpu.VMEM((256, 768), BF16),
            pltpu.SemaphoreType.DMA((9,)),
            pltpu.SemaphoreType.DMA((2,)),
            pltpu.SemaphoreType.DMA((2,)),
        ],
        compiler_params=pltpu.CompilerParams(
            collective_id=1, has_side_effects=True, vmem_limit_bytes=56 * 1024 * 1024
        ),
        name="experts",
    )(outgoing, gate_up, down)


def on_device(
    tokens, queries, suffix_keys, suffix_values, prefix_keys, prefix_values,
    out_weight, norm_gain, routes, route_weights, gate_up_weight, down_weight,
):
    rows_here, width = tokens.shape
    experts, capacity = 64, 16
    named = routes.T[:, None, :] == jnp.arange(experts, dtype=jnp.int32)[None, :, None]
    member = jnp.sum(named.astype(F32), axis=0)
    gate = jnp.sum(jnp.where(named, route_weights.T[:, None, :], 0.0), axis=0)
    before = (jnp.arange(rows_here)[:, None] < jnp.arange(rows_here)[None, :]).astype(BF16)
    rank = jnp.dot(member.astype(BF16), before, preferred_element_type=F32)
    position = jnp.where(member > 0, rank, -1.0)
    slot = jnp.arange(capacity, dtype=F32)
    place = position[:, None, :] == slot[None, :, None]
    selected = place.astype(BF16).reshape(experts * capacity, rows_here)
    weights = jnp.where(place, gate[:, None, :], 0.0)
    high = weights.astype(BF16)
    low = (weights - high.astype(F32)).astype(BF16)
    both = jnp.concatenate([high, low], axis=2)[:, None]
    both = jnp.broadcast_to(both, (experts, 2, capacity, 2 * rows_here)).reshape(-1, 2 * rows_here)

    attended, normed = attention(
        queries, prefix_keys[0], prefix_values[0], suffix_keys, suffix_values, tokens,
        norm_gain.reshape(1, width), out_weight,
    )
    outgoing = jnp.dot(selected, normed, preferred_element_type=F32).astype(BF16)
    flat = expert_rows(outgoing.reshape(experts, capacity, width), gate_up_weight[0], down_weight[0])
    parts = lax.dot_general(
        both, flat.reshape(-1, width), (((0,), (0,)), ((), ())), preferred_element_type=F32
    )
    return (attended, (parts[:rows_here] + parts[rows_here:]).astype(BF16))


def solution(mesh):
    row = P(("grp", "dev"), None)
    cube = P(("grp", "dev"), None, None)
    return jax.shard_map(
        on_device,
        mesh=mesh,
        in_specs=(row, row, row, row, P("grp", "dev", None), P("grp", "dev", None), P(), P(), row, row, cube, cube),
        out_specs=(row, row),
        check_vma=False,
    )
```

```python
import functools
import math

import jax
import jax.numpy as jnp
from jax import lax
from jax.experimental import pallas as pl
from jax.experimental.pallas import tpu as pltpu
from jax.sharding import PartitionSpec as P

HEADS = 16
HEAD_DIM = 128
TOP = 6
MESH = pl.DeviceIdType.MESH
F32 = jnp.float32
BF16 = jnp.bfloat16
NT = (((1,), (1,)), ((), ()))


def attention_kernel(
    q_ref, k_ref, v_ref, sk_ref, sv_ref, tok_ref, gain_ref, ow_hbm,
    attended_ref, normed_ref,
    qbuf, kbuf, vbuf, osend, orecv, stsend, strecv, suf_acc, suf_stat, vt, hout, resid, ow,
    recv_sem, send_sem, ow_sem,
):
    me = lax.axis_index("dev")
    y, zh, x = me // 8, (me // 4) % 2, me % 4
    head = y * 4 + x
    scale = 1.0 / math.sqrt(HEAD_DIM)

    ow_copy = pltpu.make_async_copy(ow_hbm, ow, ow_sem)
    ow_copy.start()

    barrier = pltpu.get_barrier_semaphore()

    def greet(j, c):
        pl.semaphore_signal(barrier, inc=1, device_id={"dev": (me + j) % 32}, device_id_type=MESH)
        return c

    lax.fori_loop(1, 32, greet, 0)
    pl.semaphore_wait(barrier, 31)

    def columns(h):
        return pl.ds(pl.multiple_of(h * HEAD_DIM, HEAD_DIM), HEAD_DIM)

    def key_rows(d):
        return pl.ds(pl.multiple_of(d * 32, 32), 32)

    pltpu.make_async_copy(q_ref.at[:, columns(head)], qbuf.at[head], recv_sem.at[0]).start()
    pltpu.make_async_copy(k_ref.at[:, columns(head)], kbuf.at[key_rows(me), :], recv_sem.at[1]).start()
    pltpu.make_async_copy(v_ref.at[:, columns(head)], vbuf.at[key_rows(me), :], recv_sem.at[2]).start()

    def send_kv(j, c):
        dz, dy, dx = j // 16, (j // 4) % 4, j % 4
        ty, tz, tx = (y + dy) % 4, (zh + dz) % 2, (x + dx) % 4
        to = {"dev": ty * 8 + tz * 4 + tx}
        h = ty * 4 + tx
        pltpu.make_async_remote_copy(
            k_ref.at[:, columns(h)], kbuf.at[key_rows(me), :], send_sem.at[1], recv_sem.at[1],
            device_id=to, device_id_type=MESH,
        ).start()
        pltpu.make_async_remote_copy(
            v_ref.at[:, columns(h)], vbuf.at[key_rows(me), :], send_sem.at[2], recv_sem.at[2],
            device_id=to, device_id_type=MESH,
        ).start()
        return c

    def send_q(j, c):
        ty, tx = (y + j // 4) % 4, (x + j % 4) % 4
        h = ty * 4 + tx
        pltpu.make_async_remote_copy(
            q_ref.at[:, columns(h)], qbuf.at[head], send_sem.at[0], recv_sem.at[0],
            device_id={"dev": ty * 8 + zh * 4 + tx}, device_id_type=MESH,
        ).start()
        return c

    lax.fori_loop(1, 32, send_kv, 0)
    lax.fori_loop(1, 16, send_q, 0)

    key_at = lax.broadcasted_iota(jnp.int32, (128, 128), 0)
    query_at = lax.broadcasted_iota(jnp.int32, (128, 128), 1)
    allowed = key_at <= query_at
    for h in range(HEADS):
        cols = slice(h * HEAD_DIM, (h + 1) * HEAD_DIM)
        s = lax.dot_general(sk_ref[:, cols], q_ref[:, cols], NT, preferred_element_type=F32) * scale
        s = jnp.where(allowed, s, -jnp.inf)
        m = jnp.max(s, axis=0, keepdims=True)
        p = jnp.exp(s - m)
        suf_stat[0, h : h + 1, :] = m
        suf_stat[1, h : h + 1, :] = jnp.sum(p, axis=0, keepdims=True)
        val_t = sv_ref[:, cols].astype(F32).T.astype(BF16)
        suf_acc[cols, :] = jnp.dot(val_t, p.astype(BF16), preferred_element_type=F32)

    pltpu.make_async_copy(kbuf, kbuf, recv_sem.at[1]).wait()
    pltpu.make_async_copy(vbuf, vbuf, recv_sem.at[2]).wait()
    vt[...] = vbuf[...].astype(F32).T.astype(BF16)
    pltpu.make_async_copy(qbuf, qbuf, recv_sem.at[0]).wait()

    def prefix(r, c):
        s = lax.dot_general(kbuf[...], qbuf[r], NT, preferred_element_type=F32) * scale
        m = jnp.max(s, axis=0, keepdims=True)
        p = jnp.exp(s - m)
        total = jnp.sum(p, axis=0, keepdims=True)
        acc = jnp.dot(vt[...], p.astype(BF16), preferred_element_type=F32)
        osend[r] = (acc / total).astype(BF16)
        stsend[r] = jnp.concatenate([m, total, jnp.zeros((6, 128), F32)], axis=0)
        return c

    lax.fori_loop(0, 16, prefix, 0)

    pltpu.make_async_copy(osend.at[head], orecv.at[head], recv_sem.at[3]).start()
    pltpu.make_async_copy(stsend.at[head], strecv.at[head], recv_sem.at[4]).start()

    def send_out(j, c):
        ty, tx = (y + j // 4) % 4, (x + j % 4) % 4
        to = {"dev": ty * 8 + zh * 4 + tx}
        pltpu.make_async_remote_copy(
            osend.at[ty * 4 + tx], orecv.at[head], send_sem.at[3], recv_sem.at[3],
            device_id=to, device_id_type=MESH,
        ).start()
        pltpu.make_async_remote_copy(
            stsend.at[ty * 4 + tx], strecv.at[head], send_sem.at[4], recv_sem.at[4],
            device_id=to, device_id_type=MESH,
        ).start()
        return c

    lax.fori_loop(1, 16, send_out, 0)
    pltpu.make_async_copy(strecv, strecv, recv_sem.at[4]).wait()
    pltpu.make_async_copy(orecv, orecv, recv_sem.at[3]).wait()

    for h in range(HEADS):
        cols = slice(h * HEAD_DIM, (h + 1) * HEAD_DIM)
        pre_m, pre_l = strecv[h, 0:1, :], strecv[h, 1:2, :]
        suf_m, suf_l = suf_stat[0, h : h + 1, :], suf_stat[1, h : h + 1, :]
        top = jnp.maximum(pre_m, suf_m)
        a = jnp.exp(pre_m - top) * pre_l
        b = jnp.exp(suf_m - top)
        mixed = (orecv[h].astype(F32) * a + suf_acc[cols, :] * b) / (a + suf_l * b)
        hout[:, cols] = mixed.T.astype(BF16)

    ow_copy.wait()
    square = jnp.zeros((128, 1), F32)
    for n in range(4):
        cols = slice(n * 512, (n + 1) * 512)
        att = jnp.dot(hout[...], ow[:, cols], preferred_element_type=F32).astype(BF16)
        attended_ref[:, cols] = att
        res = tok_ref[:, cols].astype(F32) + att.astype(F32)
        resid[:, cols] = res
        square = square + jnp.sum(res * res, axis=1, keepdims=True)
    factor = lax.rsqrt(square * (1.0 / 2048.0) + 1e-06)
    normed_ref[...] = (resid[...] * factor * gain_ref[...]).astype(BF16)

    pltpu.make_async_copy(qbuf.at[pl.ds(0, 15)], qbuf.at[pl.ds(0, 15)], send_sem.at[0]).wait()
    pltpu.make_async_copy(kbuf.at[pl.ds(0, 992), :], kbuf.at[pl.ds(0, 992), :], send_sem.at[1]).wait()
    pltpu.make_async_copy(vbuf.at[pl.ds(0, 992), :], vbuf.at[pl.ds(0, 992), :], send_sem.at[2]).wait()
    pltpu.make_async_copy(osend.at[pl.ds(0, 15)], osend.at[pl.ds(0, 15)], send_sem.at[3]).wait()
    pltpu.make_async_copy(stsend.at[pl.ds(0, 15)], stsend.at[pl.ds(0, 15)], send_sem.at[4]).wait()


def attention(q, k, v, sk, sv, tok, gain, ow):
    vmem = pl.BlockSpec(memory_space=pltpu.VMEM)
    return pl.pallas_call(
        attention_kernel,
        out_shape=(jax.ShapeDtypeStruct((128, 2048), BF16), jax.ShapeDtypeStruct((128, 2048), BF16)),
        in_specs=[vmem] * 7 + [pl.BlockSpec(memory_space=pl.ANY)],
        out_specs=(vmem, vmem),
        scratch_shapes=[
            pltpu.VMEM((16, 128, 128), BF16),
            pltpu.VMEM((1024, 128), BF16),
            pltpu.VMEM((1024, 128), BF16),
            pltpu.VMEM((16, 128, 128), BF16),
            pltpu.VMEM((16, 128, 128), BF16),
            pltpu.VMEM((16, 8, 128), F32),
            pltpu.VMEM((16, 8, 128), F32),
            pltpu.VMEM((2048, 128), F32),
            pltpu.VMEM((2, 16, 128), F32),
            pltpu.VMEM((128, 1024), BF16),
            pltpu.VMEM((128, 2048), BF16),
            pltpu.VMEM((128, 2048), F32),
            pltpu.VMEM((2048, 2048), BF16),
            pltpu.SemaphoreType.DMA((5,)),
            pltpu.SemaphoreType.DMA((5,)),
            pltpu.SemaphoreType.DMA,
        ],
        compiler_params=pltpu.CompilerParams(
            collective_id=0, has_side_effects=True, vmem_limit_bytes=48 * 1024 * 1024
        ),
        name="attention",
    )(q, k, v, sk, sv, tok, gain, ow)


def experts_kernel(
    out_ref, gu_hbm, down_hbm, flat_ref,
    recv, part, got, gu, down, proj, act,
    direct_sem, relay_sem, got_sem, back_sem, send_sem, weight_sem,
):
    me = lax.axis_index("grp") * 32 + lax.axis_index("dev")
    k = me // 2
    x = me % 4
    outer = ((x + 1) // 2 + 1) % 2
    gu_copy = pltpu.make_async_copy(gu_hbm, gu, weight_sem.at[0])
    down_copy = pltpu.make_async_copy(down_hbm, down, weight_sem.at[1])
    gu_copy.start()
    down_copy.start()

    def place(i):
        return {"grp": i // 32, "dev": i % 32}

    def member(q):
        return place(4 * (q // 2) + outer * 3 * (q % 2) + (1 - outer) * (1 + q % 2))

    partner = place(me + 1 - 2 * (me % 2))

    barrier = pltpu.get_barrier_semaphore()
    pl.semaphore_signal(barrier, inc=1, device_id=partner, device_id_type=MESH)

    def greet(j, c):
        pl.semaphore_signal(barrier, inc=1, device_id=member((k + j) % 64), device_id_type=MESH)
        return c

    lax.fori_loop(1, 64, greet, 0)
    pl.semaphore_wait(barrier, 64)

    pltpu.make_async_copy(out_ref.at[k], recv.at[0, 0], direct_sem.at[0]).start()

    def send(j, c):
        to = (k + j) % 64
        pltpu.make_async_remote_copy(
            out_ref.at[to], recv.at[j // 8, j % 8], send_sem.at[0], direct_sem.at[j // 8],
            device_id=member(to), device_id_type=MESH,
        ).start()
        return c

    lax.fori_loop(1, 64, send, 0)
    own, other = pl.ds(0, 8), pl.ds(8, 8)

    def relay(g):
        pltpu.make_async_copy(recv.at[g, own], recv.at[g, own], direct_sem.at[g]).wait()
        pltpu.make_async_remote_copy(
            recv.at[g, own], recv.at[g, other], send_sem.at[1], relay_sem.at[g],
            device_id=partner, device_id_type=MESH,
        ).start()

    relay(0)
    relay(1)
    gu_copy.wait()
    down_copy.wait()

    def compute(g):
        pltpu.make_async_copy(recv.at[g, other], recv.at[g, other], relay_sem.at[g]).wait()
        rows = recv[g].reshape(256, 2048)

        def project(n, c):
            cols = pl.ds(pl.multiple_of(n * 256, 256), 256)
            proj[:, cols] = jnp.dot(rows, gu[:, cols], preferred_element_type=F32)
            return c

        lax.fori_loop(0, 5, project, 0)
        proj[:, 1280:1408] = jnp.dot(rows, gu[:, 1280:1408], preferred_element_type=F32)
        whole = proj[...]
        up = pltpu.roll(whole, 704, 1)
        gate = whole[:, :768]
        act[...] = (gate / (1.0 + jnp.exp(-gate)) * up[:, :768]).astype(BF16)
        hidden = act[:, :704]

        def lower(n, c):
            cols = pl.ds(pl.multiple_of(n * 512, 512), 512)
            done = jnp.dot(hidden, down[:, cols], preferred_element_type=F32).astype(BF16)
            part[g, :, :, cols] = done.reshape(16, 16, 512)
            return c

        lax.fori_loop(0, 4, lower, 0)
        pltpu.make_async_remote_copy(
            part.at[g, other], got.at[g], send_sem.at[2], got_sem.at[g],
            device_id=partner, device_id_type=MESH,
        ).start()

    def finish(g):
        pltpu.make_async_copy(got.at[g], got.at[g], got_sem.at[g]).wait()

        def add(b, c):
            part[g, b] = (part[g, b].astype(F32) + got[g, b].astype(F32)).astype(BF16)
            return c

        lax.fori_loop(0, 8, add, 0)

    def give_back(j, c):
        pltpu.make_async_remote_copy(
            part.at[j // 8, j % 8], flat_ref.at[k], send_sem.at[3], back_sem,
            device_id=member((k + 64 - j) % 64), device_id_type=MESH,
        ).start()
        return c

    def group(g, c):
        @pl.when(g < 6)
        def _():
            relay(g + 2)

        compute(g)

        @pl.when(g == 2)
        def _():
            finish(0)
            pltpu.make_async_copy(part.at[0, 0], flat_ref.at[k], back_sem).start()
            lax.fori_loop(1, 8, give_back, 0)

        @pl.when(g > 2)
        def _():
            finish(g - 2)
            lax.fori_loop((g - 2) * 8, (g - 2) * 8 + 8, give_back, 0)

        return c

    lax.fori_loop(0, 8, group, 0)
    finish(6)
    lax.fori_loop(48, 56, give_back, 0)
    finish(7)
    lax.fori_loop(56, 64, give_back, 0)
    left = flat_ref.at[pl.ds(0, 63)]
    pltpu.make_async_copy(left, left, send_sem.at[0]).wait()
    pltpu.make_async_copy(flat_ref, flat_ref, send_sem.at[1]).wait()
    pltpu.make_async_copy(flat_ref, flat_ref, send_sem.at[2]).wait()
    pltpu.make_async_copy(left, left, send_sem.at[3]).wait()
    pltpu.make_async_copy(flat_ref, flat_ref, back_sem).wait()


def expert_rows(outgoing, gate_up, down):
    vmem = pl.BlockSpec(memory_space=pltpu.VMEM)
    hbm = pl.BlockSpec(memory_space=pl.ANY)
    return pl.pallas_call(
        experts_kernel,
        out_shape=jax.ShapeDtypeStruct((64, 16, 2048), BF16),
        in_specs=[vmem, hbm, hbm],
        out_specs=vmem,
        scratch_shapes=[
            pltpu.VMEM((8, 16, 16, 2048), BF16),
            pltpu.VMEM((8, 16, 16, 2048), BF16),
            pltpu.VMEM((8, 8, 16, 2048), BF16),
            pltpu.VMEM((2048, 1408), BF16),
            pltpu.VMEM((704, 2048), BF16),
            pltpu.VMEM((256, 1408), F32),
            pltpu.VMEM((256, 768), BF16),
            pltpu.SemaphoreType.DMA((8,)),
            pltpu.SemaphoreType.DMA((8,)),
            pltpu.SemaphoreType.DMA((8,)),
            pltpu.SemaphoreType.DMA,
            pltpu.SemaphoreType.DMA((4,)),
            pltpu.SemaphoreType.DMA((2,)),
        ],
        compiler_params=pltpu.CompilerParams(
            collective_id=1, has_side_effects=True, vmem_limit_bytes=56 * 1024 * 1024
        ),
        name="experts",
    )(outgoing, gate_up, down)


def on_device(
    tokens, queries, suffix_keys, suffix_values, prefix_keys, prefix_values,
    out_weight, norm_gain, routes, route_weights, gate_up_weight, down_weight,
):
    rows_here, width = tokens.shape
    experts, capacity = 64, 16
    named = routes.T[:, None, :] == jnp.arange(experts, dtype=jnp.int32)[None, :, None]
    member = jnp.sum(named.astype(F32), axis=0)
    gate = jnp.sum(jnp.where(named, route_weights.T[:, None, :], 0.0), axis=0)
    before = (jnp.arange(rows_here)[:, None] < jnp.arange(rows_here)[None, :]).astype(BF16)
    rank = jnp.dot(member.astype(BF16), before, preferred_element_type=F32)
    position = jnp.where(member > 0, rank, -1.0)
    slot = jnp.arange(capacity, dtype=F32)
    place = position[:, None, :] == slot[None, :, None]
    selected = place.astype(BF16).reshape(experts * capacity, rows_here)
    weights = jnp.where(place, gate[:, None, :], 0.0)
    high = weights.astype(BF16)
    low = (weights - high.astype(F32)).astype(BF16)
    both = jnp.concatenate([high, low], axis=2).reshape(experts * capacity, 2 * rows_here)

    attended, normed = attention(
        queries, prefix_keys[0], prefix_values[0], suffix_keys, suffix_values, tokens,
        norm_gain.reshape(1, width), out_weight,
    )
    outgoing = jnp.dot(selected, normed, preferred_element_type=F32).astype(BF16)
    flat = expert_rows(outgoing.reshape(experts, capacity, width), gate_up_weight[0], down_weight[0])
    parts = lax.dot_general(
        both, flat.reshape(-1, width), (((0,), (0,)), ((), ())), preferred_element_type=F32
    )
    return (attended, (parts[:rows_here] + parts[rows_here:]).astype(BF16))


def solution(mesh):
    row = P(("grp", "dev"), None)
    cube = P(("grp", "dev"), None, None)
    return jax.shard_map(
        on_device,
        mesh=mesh,
        in_specs=(row, row, row, row, P("grp", "dev", None), P("grp", "dev", None), P(), P(), row, row, cube, cube),
        out_specs=(row, row),
        check_vma=False,
    )
```

```python
import functools
import math

import jax
import jax.numpy as jnp
from jax import lax
from jax.experimental import pallas as pl
from jax.experimental.pallas import tpu as pltpu
from jax.sharding import PartitionSpec as P

HEADS = 16
HEAD_DIM = 128
TOP = 6
MESH = pl.DeviceIdType.MESH
F32 = jnp.float32
BF16 = jnp.bfloat16
NT = (((1,), (1,)), ((), ()))


def attention_kernel(
    q_hbm, k_hbm, v_hbm, sk_hbm, sv_hbm, tok_hbm, gain_ref, ow_hbm,
    attended_ref, normed_ref,
    qbuf, kbuf, vbuf, osend, orecv, stsend, strecv, suf_acc, suf_stat, vt, hout, resid, ow,
    q_ref, k_ref, v_ref, sk_ref, sv_ref, tok_ref,
    recv_sem, send_sem, ow_sem, in_sem,
):
    me = lax.axis_index("dev")
    y, zh, x = me // 8, (me // 4) % 2, me % 4
    head = y * 4 + x
    scale = 1.0 / math.sqrt(HEAD_DIM)

    ow_copy = pltpu.make_async_copy(ow_hbm, ow, ow_sem)
    pairs = ((k_hbm, k_ref), (v_hbm, v_ref), (q_hbm, q_ref), (sk_hbm, sk_ref), (sv_hbm, sv_ref), (tok_hbm, tok_ref))
    loads = [pltpu.make_async_copy(src, dst, in_sem.at[n]) for n, (src, dst) in enumerate(pairs)]
    for load in loads:
        load.start()
    ow_copy.start()

    barrier = pltpu.get_barrier_semaphore()

    def greet(j, c):
        pl.semaphore_signal(barrier, inc=1, device_id={"dev": (me + j) % 32}, device_id_type=MESH)
        return c

    lax.fori_loop(1, 32, greet, 0)
    pl.semaphore_wait(barrier, 31)

    def columns(h):
        return pl.ds(pl.multiple_of(h * HEAD_DIM, HEAD_DIM), HEAD_DIM)

    def key_rows(d):
        return pl.ds(pl.multiple_of(d * 32, 32), 32)

    for load in loads[:3]:
        load.wait()

    pltpu.make_async_copy(q_ref.at[:, columns(head)], qbuf.at[head], recv_sem.at[0]).start()
    pltpu.make_async_copy(k_ref.at[:, columns(head)], kbuf.at[key_rows(me), :], recv_sem.at[1]).start()
    pltpu.make_async_copy(v_ref.at[:, columns(head)], vbuf.at[key_rows(me), :], recv_sem.at[2]).start()

    def send_kv(j, c):
        dz, dy, dx = j // 16, (j // 4) % 4, j % 4
        ty, tz, tx = (y + dy) % 4, (zh + dz) % 2, (x + dx) % 4
        to = {"dev": ty * 8 + tz * 4 + tx}
        h = ty * 4 + tx
        pltpu.make_async_remote_copy(
            k_ref.at[:, columns(h)], kbuf.at[key_rows(me), :], send_sem.at[1], recv_sem.at[1],
            device_id=to, device_id_type=MESH,
        ).start()
        pltpu.make_async_remote_copy(
            v_ref.at[:, columns(h)], vbuf.at[key_rows(me), :], send_sem.at[2], recv_sem.at[2],
            device_id=to, device_id_type=MESH,
        ).start()
        return c

    def send_q(j, c):
        ty, tx = (y + j // 4) % 4, (x + j % 4) % 4
        h = ty * 4 + tx
        pltpu.make_async_remote_copy(
            q_ref.at[:, columns(h)], qbuf.at[head], send_sem.at[0], recv_sem.at[0],
            device_id={"dev": ty * 8 + zh * 4 + tx}, device_id_type=MESH,
        ).start()
        return c

    lax.fori_loop(1, 32, send_kv, 0)
    lax.fori_loop(1, 16, send_q, 0)

    key_at = lax.broadcasted_iota(jnp.int32, (128, 128), 0)
    query_at = lax.broadcasted_iota(jnp.int32, (128, 128), 1)
    allowed = key_at <= query_at
    for load in loads[3:]:
        load.wait()
    for h in range(HEADS):
        cols = slice(h * HEAD_DIM, (h + 1) * HEAD_DIM)
        s = lax.dot_general(sk_ref[:, cols], q_ref[:, cols], NT, preferred_element_type=F32) * scale
        s = jnp.where(allowed, s, -jnp.inf)
        m = jnp.max(s, axis=0, keepdims=True)
        p = jnp.exp(s - m)
        suf_stat[0, h : h + 1, :] = m
        suf_stat[1, h : h + 1, :] = jnp.sum(p, axis=0, keepdims=True)
        val_t = sv_ref[:, cols].astype(F32).T.astype(BF16)
        suf_acc[cols, :] = jnp.dot(val_t, p.astype(BF16), preferred_element_type=F32)

    pltpu.make_async_copy(kbuf, kbuf, recv_sem.at[1]).wait()
    pltpu.make_async_copy(vbuf, vbuf, recv_sem.at[2]).wait()
    vt[...] = vbuf[...].astype(F32).T.astype(BF16)
    pltpu.make_async_copy(qbuf, qbuf, recv_sem.at[0]).wait()

    def prefix(r, c):
        s = lax.dot_general(kbuf[...], qbuf[r], NT, preferred_element_type=F32) * scale
        m = jnp.max(s, axis=0, keepdims=True)
        p = jnp.exp(s - m)
        total = jnp.sum(p, axis=0, keepdims=True)
        acc = jnp.dot(vt[...], p.astype(BF16), preferred_element_type=F32)
        osend[r] = (acc / total).astype(BF16)
        stsend[r] = jnp.concatenate([m, total, jnp.zeros((6, 128), F32)], axis=0)
        return c

    lax.fori_loop(0, 16, prefix, 0)

    pltpu.make_async_copy(osend.at[head], orecv.at[head], recv_sem.at[3]).start()
    pltpu.make_async_copy(stsend.at[head], strecv.at[head], recv_sem.at[4]).start()

    def send_out(j, c):
        ty, tx = (y + j // 4) % 4, (x + j % 4) % 4
        to = {"dev": ty * 8 + zh * 4 + tx}
        pltpu.make_async_remote_copy(
            osend.at[ty * 4 + tx], orecv.at[head], send_sem.at[3], recv_sem.at[3],
            device_id=to, device_id_type=MESH,
        ).start()
        pltpu.make_async_remote_copy(
            stsend.at[ty * 4 + tx], strecv.at[head], send_sem.at[4], recv_sem.at[4],
            device_id=to, device_id_type=MESH,
        ).start()
        return c

    lax.fori_loop(1, 16, send_out, 0)
    pltpu.make_async_copy(strecv, strecv, recv_sem.at[4]).wait()
    pltpu.make_async_copy(orecv, orecv, recv_sem.at[3]).wait()

    for h in range(HEADS):
        cols = slice(h * HEAD_DIM, (h + 1) * HEAD_DIM)
        pre_m, pre_l = strecv[h, 0:1, :], strecv[h, 1:2, :]
        suf_m, suf_l = suf_stat[0, h : h + 1, :], suf_stat[1, h : h + 1, :]
        top = jnp.maximum(pre_m, suf_m)
        a = jnp.exp(pre_m - top) * pre_l
        b = jnp.exp(suf_m - top)
        mixed = (orecv[h].astype(F32) * a + suf_acc[cols, :] * b) / (a + suf_l * b)
        hout[:, cols] = mixed.T.astype(BF16)

    ow_copy.wait()
    square = jnp.zeros((128, 1), F32)
    for n in range(4):
        cols = slice(n * 512, (n + 1) * 512)
        att = jnp.dot(hout[...], ow[:, cols], preferred_element_type=F32).astype(BF16)
        attended_ref[:, cols] = att
        res = tok_ref[:, cols].astype(F32) + att.astype(F32)
        resid[:, cols] = res
        square = square + jnp.sum(res * res, axis=1, keepdims=True)
    factor = lax.rsqrt(square * (1.0 / 2048.0) + 1e-06)
    normed_ref[...] = (resid[...] * factor * gain_ref[...]).astype(BF16)

    pltpu.make_async_copy(qbuf.at[pl.ds(0, 15)], qbuf.at[pl.ds(0, 15)], send_sem.at[0]).wait()
    pltpu.make_async_copy(kbuf.at[pl.ds(0, 992), :], kbuf.at[pl.ds(0, 992), :], send_sem.at[1]).wait()
    pltpu.make_async_copy(vbuf.at[pl.ds(0, 992), :], vbuf.at[pl.ds(0, 992), :], send_sem.at[2]).wait()
    pltpu.make_async_copy(osend.at[pl.ds(0, 15)], osend.at[pl.ds(0, 15)], send_sem.at[3]).wait()
    pltpu.make_async_copy(stsend.at[pl.ds(0, 15)], stsend.at[pl.ds(0, 15)], send_sem.at[4]).wait()


def attention(q, k, v, sk, sv, tok, gain, ow):
    vmem = pl.BlockSpec(memory_space=pltpu.VMEM)
    return pl.pallas_call(
        attention_kernel,
        out_shape=(jax.ShapeDtypeStruct((128, 2048), BF16), jax.ShapeDtypeStruct((128, 2048), BF16)),
        in_specs=[pl.BlockSpec(memory_space=pltpu.HBM)] * 6 + [vmem, pl.BlockSpec(memory_space=pltpu.HBM)],
        out_specs=(vmem, vmem),
        scratch_shapes=[
            pltpu.VMEM((16, 128, 128), BF16),
            pltpu.VMEM((1024, 128), BF16),
            pltpu.VMEM((1024, 128), BF16),
            pltpu.VMEM((16, 128, 128), BF16),
            pltpu.VMEM((16, 128, 128), BF16),
            pltpu.VMEM((16, 8, 128), F32),
            pltpu.VMEM((16, 8, 128), F32),
            pltpu.VMEM((2048, 128), F32),
            pltpu.VMEM((2, 16, 128), F32),
            pltpu.VMEM((128, 1024), BF16),
            pltpu.VMEM((128, 2048), BF16),
            pltpu.VMEM((128, 2048), F32),
            pltpu.VMEM((2048, 2048), BF16),
            pltpu.VMEM((128, 2048), BF16),
            pltpu.VMEM((32, 2048), BF16),
            pltpu.VMEM((32, 2048), BF16),
            pltpu.VMEM((128, 2048), BF16),
            pltpu.VMEM((128, 2048), BF16),
            pltpu.VMEM((128, 2048), BF16),
            pltpu.SemaphoreType.DMA((5,)),
            pltpu.SemaphoreType.DMA((5,)),
            pltpu.SemaphoreType.DMA,
            pltpu.SemaphoreType.DMA((6,)),
        ],
        compiler_params=pltpu.CompilerParams(
            collective_id=0, has_side_effects=True, vmem_limit_bytes=67_043_328
        ),
        name="attention",
    )(q, k, v, sk, sv, tok, gain, ow)


def experts_kernel(
    out_ref, gu_hbm, down_hbm, flat_ref,
    recv, part, got, gu, down, proj, act,
    direct_sem, relay_sem, got_sem, back_sem, send_sem, weight_sem,
):
    me = lax.axis_index("grp") * 32 + lax.axis_index("dev")
    k = me // 2
    x = me % 4
    outer = ((x + 1) // 2 + 1) % 2
    gu_copy = pltpu.make_async_copy(gu_hbm, gu, weight_sem.at[0])
    down_copy = pltpu.make_async_copy(down_hbm, down, weight_sem.at[1])
    gu_copy.start()
    down_copy.start()

    def place(i):
        return {"grp": i // 32, "dev": i % 32}

    def member(q):
        return place(4 * (q // 2) + outer * 3 * (q % 2) + (1 - outer) * (1 + q % 2))

    partner = place(me + 1 - 2 * (me % 2))

    barrier = pltpu.get_barrier_semaphore()
    pl.semaphore_signal(barrier, inc=1, device_id=partner, device_id_type=MESH)

    def greet(j, c):
        pl.semaphore_signal(barrier, inc=1, device_id=member((k + j) % 64), device_id_type=MESH)
        return c

    lax.fori_loop(1, 64, greet, 0)
    pl.semaphore_wait(barrier, 64)

    pltpu.make_async_copy(out_ref.at[k], recv.at[0, 0], direct_sem.at[0]).start()

    def send(j, c):
        to = (k + j) % 64
        pltpu.make_async_remote_copy(
            out_ref.at[to], recv.at[j // 8, j % 8], send_sem.at[0], direct_sem.at[j // 8],
            device_id=member(to), device_id_type=MESH,
        ).start()
        return c

    lax.fori_loop(1, 64, send, 0)
    own, other = pl.ds(0, 8), pl.ds(8, 8)

    def relay(g):
        pltpu.make_async_copy(recv.at[g, own], recv.at[g, own], direct_sem.at[g]).wait()
        pltpu.make_async_remote_copy(
            recv.at[g, own], recv.at[g, other], send_sem.at[1], relay_sem.at[g],
            device_id=partner, device_id_type=MESH,
        ).start()

    relay(0)
    relay(1)
    gu_copy.wait()
    down_copy.wait()

    def compute(g):
        pltpu.make_async_copy(recv.at[g, other], recv.at[g, other], relay_sem.at[g]).wait()
        rows = recv[g].reshape(256, 2048)

        def project(n, c):
            cols = pl.ds(pl.multiple_of(n * 256, 256), 256)
            proj[:, cols] = jnp.dot(rows, gu[:, cols], preferred_element_type=F32)
            return c

        lax.fori_loop(0, 5, project, 0)
        proj[:, 1280:1408] = jnp.dot(rows, gu[:, 1280:1408], preferred_element_type=F32)
        whole = proj[...]
        up = pltpu.roll(whole, 704, 1)
        gate = whole[:, :768]
        act[...] = (gate / (1.0 + jnp.exp(-gate)) * up[:, :768]).astype(BF16)
        hidden = act[:, :704]

        def lower(n, c):
            cols = pl.ds(pl.multiple_of(n * 512, 512), 512)
            done = jnp.dot(hidden, down[:, cols], preferred_element_type=F32).astype(BF16)
            part[g, :, :, cols] = done.reshape(16, 16, 512)
            return c

        lax.fori_loop(0, 4, lower, 0)
        pltpu.make_async_remote_copy(
            part.at[g, other], got.at[g], send_sem.at[2], got_sem.at[g],
            device_id=partner, device_id_type=MESH,
        ).start()

    def finish(g):
        pltpu.make_async_copy(got.at[g], got.at[g], got_sem.at[g]).wait()

        def add(b, c):
            part[g, b] = (part[g, b].astype(F32) + got[g, b].astype(F32)).astype(BF16)
            return c

        lax.fori_loop(0, 8, add, 0)

    def give_back(j, c):
        pltpu.make_async_remote_copy(
            part.at[j // 8, j % 8], flat_ref.at[k], send_sem.at[3], back_sem,
            device_id=member((k + 64 - j) % 64), device_id_type=MESH,
        ).start()
        return c

    def group(g, c):
        @pl.when(g < 6)
        def _():
            relay(g + 2)

        compute(g)

        @pl.when(g == 2)
        def _():
            finish(0)
            pltpu.make_async_copy(part.at[0, 0], flat_ref.at[k], back_sem).start()
            lax.fori_loop(1, 8, give_back, 0)

        @pl.when(g > 2)
        def _():
            finish(g - 2)
            lax.fori_loop((g - 2) * 8, (g - 2) * 8 + 8, give_back, 0)

        return c

    lax.fori_loop(0, 8, group, 0)
    finish(6)
    lax.fori_loop(48, 56, give_back, 0)
    finish(7)
    lax.fori_loop(56, 64, give_back, 0)
    left = flat_ref.at[pl.ds(0, 63)]
    pltpu.make_async_copy(left, left, send_sem.at[0]).wait()
    pltpu.make_async_copy(flat_ref, flat_ref, send_sem.at[1]).wait()
    pltpu.make_async_copy(flat_ref, flat_ref, send_sem.at[2]).wait()
    pltpu.make_async_copy(left, left, send_sem.at[3]).wait()
    pltpu.make_async_copy(flat_ref, flat_ref, back_sem).wait()


def expert_rows(outgoing, gate_up, down):
    vmem = pl.BlockSpec(memory_space=pltpu.VMEM)
    hbm = pl.BlockSpec(memory_space=pl.ANY)
    return pl.pallas_call(
        experts_kernel,
        out_shape=jax.ShapeDtypeStruct((64, 16, 2048), BF16),
        in_specs=[vmem, hbm, hbm],
        out_specs=vmem,
        scratch_shapes=[
            pltpu.VMEM((8, 16, 16, 2048), BF16),
            pltpu.VMEM((8, 16, 16, 2048), BF16),
            pltpu.VMEM((8, 8, 16, 2048), BF16),
            pltpu.VMEM((2048, 1408), BF16),
            pltpu.VMEM((704, 2048), BF16),
            pltpu.VMEM((256, 1408), F32),
            pltpu.VMEM((256, 768), BF16),
            pltpu.SemaphoreType.DMA((8,)),
            pltpu.SemaphoreType.DMA((8,)),
            pltpu.SemaphoreType.DMA((8,)),
            pltpu.SemaphoreType.DMA,
            pltpu.SemaphoreType.DMA((4,)),
            pltpu.SemaphoreType.DMA((2,)),
        ],
        compiler_params=pltpu.CompilerParams(
            collective_id=1, has_side_effects=True, vmem_limit_bytes=56 * 1024 * 1024
        ),
        name="experts",
    )(outgoing, gate_up, down)


def on_device(
    tokens, queries, suffix_keys, suffix_values, prefix_keys, prefix_values,
    out_weight, norm_gain, routes, route_weights, gate_up_weight, down_weight,
):
    rows_here, width = tokens.shape
    experts, capacity = 64, 16
    named = routes.T[:, None, :] == jnp.arange(experts, dtype=jnp.int32)[None, :, None]
    member = jnp.sum(named.astype(F32), axis=0)
    gate = jnp.sum(jnp.where(named, route_weights.T[:, None, :], 0.0), axis=0)
    before = (jnp.arange(rows_here)[:, None] < jnp.arange(rows_here)[None, :]).astype(BF16)
    rank = jnp.dot(member.astype(BF16), before, preferred_element_type=F32)
    position = jnp.where(member > 0, rank, -1.0)
    slot = jnp.arange(capacity, dtype=F32)
    place = position[:, None, :] == slot[None, :, None]
    selected = place.astype(BF16).reshape(experts * capacity, rows_here)
    weights = jnp.where(place, gate[:, None, :], 0.0)
    high = weights.astype(BF16)
    low = (weights - high.astype(F32)).astype(BF16)
    both = jnp.concatenate([high, low], axis=2).reshape(experts * capacity, 2 * rows_here)

    attended, normed = attention(
        queries, prefix_keys[0], prefix_values[0], suffix_keys, suffix_values, tokens,
        norm_gain.reshape(1, width), out_weight,
    )
    outgoing = jnp.dot(selected, normed, preferred_element_type=F32).astype(BF16)
    flat = expert_rows(outgoing.reshape(experts, capacity, width), gate_up_weight[0], down_weight[0])
    parts = lax.dot_general(
        both, flat.reshape(-1, width), (((0,), (0,)), ((), ())), preferred_element_type=F32
    )
    return (attended, (parts[:rows_here] + parts[rows_here:]).astype(BF16))


def solution(mesh):
    row = P(("grp", "dev"), None)
    cube = P(("grp", "dev"), None, None)
    return jax.shard_map(
        on_device,
        mesh=mesh,
        in_specs=(row, row, row, row, P("grp", "dev", None), P("grp", "dev", None), P(), P(), row, row, cube, cube),
        out_specs=(row, row),
        check_vma=False,
    )
```
